32 devices in a mesh: cube: 2 (over x), chan: 8 (over z, y), split: 2 (over core).
Axes of the slice: x: 2, y: 2, z: 4, core: 2. Of those that a mesh axis runs over, the one named last changes fastest.
Arguments:
- sky_image: bfloat16 [16, 8, 1, 2, 512, 128], P(('cube', 'chan'), None, None, 'split'), parts along dimension 0, may hold values from 0 to 8
- dirty_image: bfloat16 [16, 8, 1, 2, 512, 128], P(('cube', 'chan'), None, None, 'split'), parts along dimension 0, may hold values from -6 to 6
- uv_weights: int32 [16, 1024, 512], P(('cube', 'chan'), 'split'), parts along dimension 0, may hold values from 0 to 7
- dual_coeffs: bfloat16 [4, 16, 8, 2, 512, 128], P(None, 'cube', 'chan', 'split'), parts along dimension 1, may hold values from -3 to 3
- support_mask: int32 [8, 2, 512, 128], P('chan', 'split'), may hold values 0 or 1
- row_taps: float32 [4, 17], replicated, may hold values from -1.5 to 1.5
- col_taps: float32 [4, 17], replicated, may hold values from -1.5 to 1.5
Outputs:
- new_image: bfloat16 [16, 8, 1, 2, 512, 128], P(('cube', 'chan'), None, None, 'split'), parts along dimension 0
- new_dual: bfloat16 [4, 16, 8, 2, 512, 128], P(None, 'cube', 'chan', 'split'), parts along dimension 1
The draws below stay inside these ranges and needn't reach their ends.
There are 2 independent parts, one for each index of `cube`. The reference program is written for one: setup_inputs(seed, part) draws one part's arguments, and reference() takes and returns one part's arrays. A program takes and returns all parts, laid end to end along the dimension named above; an argument that names none is the same for every part. Nothing has to cross between parts.
All inputs are finite; a program needn't handle non-finite values. No bound on the sum of `support_mask` on one device may be relied on, other than what follows from the above.
Results may differ from the reference program's by a relative error of at most 0.015.
Values may be sent and summed in bfloat16 or wider, within the bound.
A program may use at most 128 MiB of HBM per device.

```python
import math
import jax
import jax.numpy as jnp
from jax import lax

NPIX = 1024
FCOLS = 8
NB = 4
MARGIN = 8
TAPS = 17
CH = 8
FACETS = 8
FROWS = 1
FS = 128
SR = 512
HALF = 512


def draw_sky_image(key, part):
    full_shape = (CH, FCOLS, FROWS, 2, SR, FS)
    key_space = jax.random.fold_in(key, 12)
    key_fresh = jax.random.fold_in(key, 13)
    key_jitter = jax.random.fold_in(key, 14)
    channel_ramp = jnp.arange(CH, dtype=jnp.float32) / max(CH - 1, 1)
    fresh = jax.random.uniform(key_fresh, full_shape, jnp.float32, 0.0, 2.0)
    jitter = jnp.exp(jax.random.uniform(key_jitter, (CH,), jnp.float32, -0.2, 0.2))
    channel_scale = 0.15 * jnp.exp(channel_ramp * math.log(10.0)) * jitter
    spatial = jnp.exp(jax.random.uniform(key_space, full_shape[1:], jnp.float32, -math.log(3.0), math.log(3.0)))
    values = channel_scale[:, None, None, None, None, None] * spatial[None] * fresh
    return jnp.minimum(values, 8.0).astype(jnp.bfloat16)


def place_ends(result, own_key, smallest, largest):
    dims = result.shape
    spot = [jax.random.randint(jax.random.fold_in(own_key, axis), (), 0, dims[axis]) for axis in range(len(dims))]
    result = result.at[tuple(spot)].set(smallest)
    longest = dims.index(max(dims))
    spot[longest] = (spot[longest] + 1) % dims[longest]
    return result.at[tuple(spot)].set(largest)


def block_scale(stream_key, dims, pieces, low, largest):
    factor_of, own = 1.0, jax.random.fold_in(stream_key, 6)
    for axis_at, shards_of in pieces:
        heights = jnp.exp(jax.random.uniform(jax.random.fold_in(own, axis_at), (shards_of,), jnp.float32, low / len(pieces), largest / len(pieces)))
        factor_of = factor_of * jnp.repeat(heights, dims[axis_at] // shards_of).reshape([-1 if axis == axis_at else 1 for axis in range(len(dims))])
    return factor_of


def centred(stream_key, shape, scale, reach, shards=(), kind=jnp.bfloat16):
    entries = jax.random.normal(stream_key, shape, jnp.float32) * scale
    if len(shards) > 0:
        entries = block_scale(stream_key, shape, shards, -0.22, 0.18) * entries
    return jnp.clip(entries, min=-reach, max=reach).astype(kind)


def setup_inputs(seed: int = 0, part: int = 0) -> dict:
    streams_of = jax.random.split(jax.random.key(seed), 8)
    part_keys = jax.random.split(jax.random.fold_in(streams_of[7], part), 8)
    sky_image = draw_sky_image(jax.random.fold_in(jax.random.fold_in(streams_of[7], part), 71), part)
    dirty_image = centred(part_keys[1], (CH, FCOLS, FROWS, 2, SR, FS), 1.0, 6.0, ((0, 8), (3, 2)))
    uv_weights = place_ends(jax.random.randint(part_keys[2], (CH, NPIX, HALF), 0, 8), jax.random.fold_in(part_keys[2], 1), 0, 7).astype(jnp.int32)
    dual_coeffs = centred(part_keys[3], (NB, CH, FACETS, 2, SR, FS), 0.5, 3.0, ((2, 8), (3, 2)))
    support_mask = place_ends((jax.random.randint(streams_of[4], (FACETS, 2, SR, FS), 0, 4) < 3).astype(jnp.int32), jax.random.fold_in(streams_of[4], 1), 0, 1)
    row_taps = centred(streams_of[5], (NB, TAPS), TAPS ** -0.5, 1.5, (), jnp.float32)
    col_taps = centred(streams_of[6], (NB, TAPS), TAPS ** -0.5, 1.5, (), jnp.float32)
    return dict(sky_image=sky_image, dirty_image=dirty_image, uv_weights=uv_weights, dual_coeffs=dual_coeffs, support_mask=support_mask, row_taps=row_taps, col_taps=col_taps)


primal_step = 0.5
dual_step = 0.5
radius = 6.0
weight_unit = 0.25

def dft_block(out_rows, in_rows):
    product = out_rows[:, None] * in_rows[None, :] % NPIX
    phases = product.astype(jnp.float32) * (2.0 * math.pi / NPIX)
    factor = 1.0 / math.sqrt(NPIX)
    return ((jnp.cos(phases) * factor).astype(jnp.bfloat16), (-jnp.sin(phases) * factor).astype(jnp.bfloat16))

def to_full(blocks, leading):
    count = len(leading)
    shaped = blocks.reshape(leading + (FCOLS, FROWS, 2, SR, FS))
    axes_order = tuple(range(count)) + (count + 1, count + 2, count + 3, count, count + 4)
    return shaped.transpose(axes_order).reshape(leading + (NPIX, NPIX))

def from_full(full, leading, target):
    count = len(leading)
    shaped = full.reshape(leading + (FROWS, 2, SR, FCOLS, FS))
    axes_order = tuple(range(count)) + (count + 3, count, count + 1, count + 2, count + 4)
    return shaped.transpose(axes_order).reshape(target)

def filter_axis(values, tap_values, axis, adjoint):
    as_float = values.astype(jnp.float32)
    padding = [(0, 0)] * as_float.ndim
    padding[axis] = (MARGIN, MARGIN)
    padded = jnp.pad(as_float, padding)
    extent = as_float.shape[axis]
    summed = jnp.zeros_like(as_float)
    for tap_index in range(TAPS):
        offset = 2 * MARGIN - tap_index if adjoint else tap_index
        summed = summed + tap_values[tap_index].astype(jnp.float32) * lax.slice_in_dim(padded, offset, offset + extent, axis=axis)
    return summed

def reference(sky_image, dirty_image, uv_weights, dual_coeffs, support_mask, row_taps, col_taps):
    pixel_index = jnp.arange(NPIX, dtype=jnp.int32)
    freq_index = jnp.arange(HALF, dtype=jnp.int32)
    cx_re, cx_im = dft_block(freq_index, pixel_index)
    cy_re, cy_im = dft_block(pixel_index, pixel_index)

    def channel_gradient(pair):
        picture, counts = pair
        half_re = jnp.dot(picture, cx_re.T, preferred_element_type=jnp.float32).astype(jnp.bfloat16)
        half_im = jnp.dot(picture, cx_im.T, preferred_element_type=jnp.float32).astype(jnp.bfloat16)
        vis_re = jnp.dot(cy_re, half_re, preferred_element_type=jnp.float32) - jnp.dot(cy_im, half_im, preferred_element_type=jnp.float32)
        vis_im = jnp.dot(cy_re, half_im, preferred_element_type=jnp.float32) + jnp.dot(cy_im, half_re, preferred_element_type=jnp.float32)
        weight_scale = weight_unit * counts.astype(jnp.float32)
        res_re = (weight_scale * vis_re).astype(jnp.bfloat16)
        res_im = (weight_scale * vis_im).astype(jnp.bfloat16)
        back_re = (jnp.dot(cy_re.T, res_re, preferred_element_type=jnp.float32) + jnp.dot(cy_im.T, res_im, preferred_element_type=jnp.float32)).astype(jnp.bfloat16)
        back_im = (jnp.dot(cy_re.T, res_im, preferred_element_type=jnp.float32) - jnp.dot(cy_im.T, res_re, preferred_element_type=jnp.float32)).astype(jnp.bfloat16)
        return jnp.dot(back_re, cx_re, preferred_element_type=jnp.float32) + jnp.dot(back_im, cx_im, preferred_element_type=jnp.float32)
    picture = to_full(sky_image, (CH,))
    dirty = to_full(dirty_image, (CH,)).astype(jnp.float32)
    gradient = lax.map(channel_gradient, (picture, uv_weights))
    row_bf = row_taps.astype(jnp.bfloat16)
    col_bf = col_taps.astype(jnp.bfloat16)
    dual_full = to_full(dual_coeffs, (NB, CH))
    adjoint = jnp.zeros((CH, NPIX, NPIX), jnp.float32)
    for basis in range(NB):
        along = filter_axis(dual_full[basis], col_bf[basis], 2, True).astype(jnp.bfloat16)
        adjoint = adjoint + filter_axis(along, row_bf[basis], 1, True)
    adjoint_rounded = lax.optimization_barrier(adjoint.astype(jnp.bfloat16)).astype(jnp.float32)
    updated = jnp.maximum(picture.astype(jnp.float32) - primal_step * (gradient - dirty + adjoint_rounded), 0.0)
    new_full = updated.astype(jnp.bfloat16)
    extrapolated = (2.0 * new_full.astype(jnp.float32) - picture.astype(jnp.float32)).astype(jnp.bfloat16)
    keep_mask = to_full(support_mask, ()).astype(jnp.float32)
    duals = []
    for basis in range(NB):
        along = filter_axis(extrapolated, col_bf[basis], 2, False).astype(jnp.bfloat16)
        coefficients = filter_axis(along, row_bf[basis], 1, False)
        stepped = dual_full[basis].astype(jnp.float32) + dual_step * coefficients
        length = jnp.sqrt(lax.optimization_barrier(jnp.sum(stepped * stepped, axis=0)))
        shrink = radius * keep_mask / jnp.maximum(length, radius)
        duals.append((stepped * shrink[None]).astype(jnp.bfloat16))
    new_dual = from_full(jnp.stack(duals), (NB, CH), (NB, CH, FACETS, 2, SR, FS))
    new_image = from_full(new_full, (CH,), (CH, FCOLS, FROWS, 2, SR, FS))
    return (new_image, new_dual)
```

```python
import functools
import math

import jax
import jax.numpy as jnp
import numpy as np
from jax import lax
from jax.experimental import pallas as pl
from jax.experimental.pallas import tpu as pltpu
from jax.sharding import PartitionSpec as P

NB = 4
TAPS = 17
MARGIN = 8
PAD = 16

primal_step = 0.5
dual_step = 0.5
radius = 6.0
weight_unit = 0.25
f32 = jnp.float32
bf16 = jnp.bfloat16


def dot(a, b):
    return jnp.dot(a, b, preferred_element_type=f32)


def col_dft(npix):
    half = npix // 2
    product = np.arange(npix)[:, None] * np.arange(half)[None, :] % npix
    phases = product.astype(np.float32) * np.float32(2.0 * math.pi / npix)
    factor = np.float32(1.0 / math.sqrt(npix))
    table = np.concatenate([np.cos(phases) * factor, -np.sin(phases) * factor], axis=1)
    return jnp.asarray(table.astype(jnp.bfloat16))


def bands(index, taps):
    outs = [jnp.zeros(index.shape, f32) for _ in range(NB)]
    for t in range(TAPS):
        hit = index == t
        outs = [jnp.where(hit, taps[n, t], outs[n]) for n in range(NB)]
    return [o.astype(bf16) for o in outs]


def adjoint_tables(W, B, row_taps, col_taps, gcols, gside, hrows):
    per = W // (2 * MARGIN)
    span = B + 2 * PAD
    i = lax.broadcasted_iota(jnp.int32, (W, W), 0)
    j = lax.broadcasted_iota(jnp.int32, (W, W), 1)
    main_bands = bands(j - i + MARGIN, col_taps)
    jj = j % (W // 2)
    side = jnp.where(j < W // 2, jj - MARGIN, W + jj)
    side_bands = bands(jnp.where(jj < MARGIN, side - i + MARGIN, -1), col_taps)
    for n in range(NB):
        none = jnp.zeros((W, W), bf16)
        gcols[n, :W, :W] = main_bands[n]
        gcols[n, :W, W:] = none
        gcols[n, W:, :W] = none
        gcols[n, W:, W:] = main_bands[n]
        table = side_bands[n].astype(f32)
        for cc in range(per):
            moved = pltpu.roll(table, cc * MARGIN, 1) if cc else table
            gside[n, cc * W : (cc + 1) * W] = moved.astype(bf16)
    r = lax.broadcasted_iota(jnp.int32, (B, NB * span), 0)
    w = lax.broadcasted_iota(jnp.int32, (B, NB * span), 1)
    basis = lax.broadcasted_iota(jnp.int32, (1, NB * span), 1) // span
    index = r - w % span + PAD + MARGIN
    out = jnp.zeros(index.shape, f32)
    for t in range(TAPS):
        tap = jnp.full(basis.shape, row_taps[0, t], f32)
        for n in range(1, NB):
            tap = jnp.where(basis == n, row_taps[n, t], tap)
        out = jnp.where(index == t, tap, out)
    hrows[...] = out.astype(bf16)


def forward_tables(W, B, row_taps, col_taps, fcols, frows):
    i = lax.broadcasted_iota(jnp.int32, (W, W), 0)
    j = lax.broadcasted_iota(jnp.int32, (W, W), 1)
    main_bands = bands(i - j + MARGIN, col_taps)
    k = lax.broadcasted_iota(jnp.int32, (2 * MARGIN, W), 0)
    jk = lax.broadcasted_iota(jnp.int32, (2 * MARGIN, W), 1)
    side = jnp.where(k < MARGIN, k - MARGIN, W - MARGIN + k)
    side_bands = bands(side - jk + MARGIN, col_taps)
    r = lax.broadcasted_iota(jnp.int32, (B, B + 2 * PAD), 0)
    w = lax.broadcasted_iota(jnp.int32, (B, B + 2 * PAD), 1)
    row_bands = bands(w - r - PAD + MARGIN, row_taps)
    for n in range(NB):
        fcols[:W, n * W : (n + 1) * W] = main_bands[n]
        fcols[W:, n * W : (n + 1) * W] = side_bands[n]
        frows[n] = row_bands[n]


def spill_cols(R, group, per, u, up, lo, gside, dcs, halo):
    for n in range(NB):
        table = gside[n]
        if halo:
            top = jnp.concatenate([up[n, group * per + cc] for cc in range(per)], axis=1)
            bottom = jnp.concatenate([lo[n, group * per + cc] for cc in range(per)], axis=1)
            out = dot(jnp.concatenate([top, bottom], axis=0), table).astype(bf16)
            dcs[n, :PAD] = out[:PAD]
            dcs[n, PAD + R :] = out[PAD:]
        else:
            rows = jnp.concatenate([u[n, group * per + cc] for cc in range(per)], axis=1)
            dcs[n, PAD : PAD + R] = dot(rows, table).astype(bf16)


def stack_rows(buf, k, B):
    span = B + 2 * PAD
    return jnp.concatenate([buf[n, k * B : k * B + span] for n in range(NB)], axis=0)


def spill_rows(R, B, group, hrows, dcs, spout):
    for k in range(R // B):
        spout[group, :, k * B : k * B + B] = dot(hrows[...], stack_rows(dcs, k, B)).T.astype(bf16)


def place_sides(W, cc):
    row = lax.broadcasted_iota(jnp.int32, (W, W), 0)
    col = lax.broadcasted_iota(jnp.int32, (W, W), 1)
    rr = row % (W // 2)
    target = jnp.where(row < W // 2, 0, W - MARGIN) + rr % MARGIN
    return jnp.where((rr // MARGIN == cc) & (col == target), 1.0, 0.0).astype(bf16)


def adjoint_pair(R, W, B, chans, u, up, lo, gcols, hrows, sides, dc, store):
    per = W // (2 * MARGIN)
    for n in range(NB):
        rows = [jnp.concatenate([up[n, c], u[n, c], lo[n, c]], axis=0) for c in chans]
        dc[n] = dot(jnp.concatenate(rows, axis=1), gcols[n]).astype(bf16)
    place = [place_sides(W, c % per) for c in chans]
    for k in range(R // B):
        out = dot(hrows[...], stack_rows(dc, k, B))
        for e, c in enumerate(chans):
            moved = dot(sides[c // per, k * B : k * B + B], place[e])
            store(e, k, (out[:, e * W : (e + 1) * W] + moved).astype(bf16))


def half_chunk(FC, x, colT, out, lanes):
    rows = jnp.concatenate([x[b] for b in range(FC)], axis=1)
    out[:, lanes] = dot(rows, colT[:, lanes]).astype(bf16)


def table_body(s, FR, R, colT, bown, aown, aoth):
    half = FR * R
    for a in range(FR):
        own = pl.ds(pl.multiple_of((2 * a + s) * R, R), R)
        bown[a * R : (a + 1) * R] = colT[own, :]
    odd_lane = lax.broadcasted_iota(jnp.int32, (1, half), 1) % 2 == 1
    flip = jnp.where(odd_lane & (s == 1), -1.0, 1.0).astype(f32)
    odd_row = lax.broadcasted_iota(jnp.int32, (half, 1), 0) % 2 == 1
    for dst, part in ((aown, s), (aoth, 1 - s)):
        for q in range(2):
            lanes = slice(q * half, (q + 1) * half)
            if FR == 1:
                sign = jnp.where(odd_row & (part == 1), -1.0, 1.0).astype(f32)
                dst[:, lanes] = (colT[:half, lanes].astype(f32) * (sign * flip)).astype(bf16)
                continue
            pieces = [
                colT[pl.ds(pl.multiple_of((2 * a + part) * R, R), R), lanes] for a in range(FR)
            ]
            block = jnp.concatenate(pieces, axis=0)
            dst[:, lanes] = (block.astype(f32).T * flip).astype(bf16)


def stack_re_im(ref, lanes_re, lanes_im, transpose):
    re, im = ref[:, lanes_re], ref[:, lanes_im]
    if transpose:
        return jnp.concatenate([re, im], 0), jnp.concatenate([im, -re], 0)
    return jnp.concatenate([re, -im], 0), jnp.concatenate([im, re], 0)


def vis_chunk(aown, aoth, hown, hoth, wts, out, re_l, im_l):
    own_re, own_im = stack_re_im(hown, re_l, im_l, False)
    oth_re, oth_im = stack_re_im(hoth, re_l, im_l, False)
    scale = weight_unit * wts[:, re_l].astype(f32)
    re = dot(aown[...], own_re) + dot(aoth[...], oth_re)
    out[:, re_l] = (scale * re).astype(bf16)
    im = dot(aown[...], own_im) + dot(aoth[...], oth_im)
    out[:, im_l] = (scale * im).astype(bf16)


def back_chunk(s, half, bown, wown, woth, out, re_l, im_l):
    odd = lax.broadcasted_iota(jnp.int32, (half, 1), 0) % 2 == 1
    own_sign = jnp.where(odd & (s == 1), -1.0, 1.0)
    oth_sign = jnp.where(odd & (s == 0), -1.0, 1.0)
    own_re, own_im = stack_re_im(wown, re_l, im_l, True)
    oth_re, oth_im = stack_re_im(woth, re_l, im_l, True)
    re = own_sign * dot(bown[...], own_re) + oth_sign * dot(bown[...], oth_re)
    out[:, re_l] = re.astype(bf16)
    im = own_sign * dot(bown[...], own_im) + oth_sign * dot(bown[...], oth_im)
    out[:, im_l] = im.astype(bf16)


def gradient_body(FC, W, back, colT, x, d, pre):
    step = 2 * W

    @pl.loop(0, FC // 2)
    def _(j):
        lanes = pl.ds(pl.multiple_of(j * step, step), step)
        grad = lax.dot_general(
            back[...], colT[lanes, :], (((1,), (1,)), ((), ())), preferred_element_type=f32
        )
        xs = jnp.concatenate([x[2 * j], x[2 * j + 1]], axis=1).astype(f32)
        ds = jnp.concatenate([d[2 * j], d[2 * j + 1]], axis=1).astype(f32)
        pre[:, lanes] = xs - primal_step * (grad - ds)


def forward_cols(R, W, c, main, sides, fcols, ic):
    out = dot(main[c], fcols[:W]) + lax.dot_general(
        sides[c], fcols[W:], (((0,), (0,)), ((), ())), preferred_element_type=f32
    )
    lanes = pl.ds(pl.multiple_of(c * W, W), W)
    for n in range(NB):
        ic[n, PAD : PAD + R, lanes] = out[:, n * W : (n + 1) * W].astype(bf16)


def forward_rows(R, W, B, chans, first, ic, frows, u, total):
    span = B + 2 * PAD
    lanes = [pl.ds(pl.multiple_of(c * W, W), W) for c in chans]
    for n in range(NB):
        for k in range(R // B):
            rows = slice(k * B, (k + 1) * B)
            block = [ic[n, k * B : k * B + span, at] for at in lanes]
            coef = dot(frows[n], jnp.concatenate(block, axis=1) if len(block) > 1 else block[0])
            acc = None if first else total[n, rows]
            for e, c in enumerate(chans):
                st = u[n, c, rows].astype(f32) + dual_step * coef[:, e * W : (e + 1) * W]
                u[n, c, rows] = st.astype(bf16)
                acc = st * st if acc is None else acc + st * st
            total[n, rows] = acc


def shrink_body(C, R, W, B, st, total, mask, new_in, out_hbm, new_hbm, out, sem_new, sem):
    moved = pltpu.make_async_copy(new_in, new_hbm, sem_new)
    moved.start()
    copies = []
    for n in range(NB):
        for k in range(R // B):
            rows = slice(k * B, (k + 1) * B)
            keep = radius * mask[rows].astype(f32)
            scale = keep / jnp.maximum(jnp.sqrt(total[n, rows]), radius)
            for c in range(C):
                out[n, c, rows] = (st[n, c, rows].astype(f32) * scale).astype(bf16)
        copy = pltpu.make_async_copy(out.at[n], out_hbm.at[n], sem.at[n])
        copy.start()
        copies.append(copy)
    for copy in copies:
        copy.wait()
    moved.wait()


def step_kernel(
    C, FC, FR, R, W, B,
    u_hbm, x_hbm, d_hbm, wts_hbm, mask_hbm, colT_hbm, row_taps, col_taps,
    new, u, total, mask,
    x, d, wts, colT, gcols, gside, hrows, fcols, frows,
    up, lo, dc, dcs, spout, spin, sides, adj, radj,
    hown, hoth, wown, woth, back, bown, aown, aoth, pre,
    ext, exts, rmain, rsides, ic,
    send_u, recv_u, send_s, recv_s, send_a, recv_a,
    send_e, recv_e, send_es, recv_es, send_p, recv_p, send_h, recv_h, load,
):
    half = FC * W // 2
    me = lax.axis_index("chan")
    s = lax.axis_index("split")
    ma, mb = me % FR, me // FR
    has_up = (ma > 0) | (s == 1)
    has_down = (ma < FR - 1) | (s == 0)
    partner = {"chan": me, "split": 1 - s}
    down_id = {"chan": (me + s) % C, "split": 1 - s}
    up_id = {"chan": (me + s + C - 1) % C, "split": 1 - s}
    left_id = {"chan": (me + C - FR) % C, "split": s}
    right_id = {"chan": (me + FR) % C, "split": s}
    per = W // (2 * MARGIN)
    groups = C // per

    def remote(src, dst, ssem, rsem, device):
        return pltpu.make_async_remote_copy(
            src_ref=src, dst_ref=dst, send_sem=ssem, recv_sem=rsem,
            device_id=device, device_id_type=pl.DeviceIdType.MESH,
        )

    loads = [
        pltpu.make_async_copy(a, b, load.at[i])
        for i, (a, b) in enumerate(
            [(u_hbm, u), (x_hbm, x), (colT_hbm, colT), (wts_hbm, wts), (d_hbm, d), (mask_hbm, mask)]
        )
    ]
    for copy in loads:
        copy.start()
    barrier = pltpu.get_barrier_semaphore()

    @pl.loop(1, C)
    def _(i):
        pl.semaphore_signal(
            barrier, inc=1, device_id={"chan": (me + i) % C, "split": s},
            device_id_type=pl.DeviceIdType.MESH,
        )

    pl.semaphore_signal(barrier, inc=1, device_id=partner, device_id_type=pl.DeviceIdType.MESH)
    if FR > 1:
        cross = jnp.where(s == 0, ma > 0, ma < FR - 1)
        cross_chan = jnp.where(s == 0, (me + C - 1) % C, (me + 1) % C)

        @pl.when(cross)
        def _():
            pl.semaphore_signal(
                barrier, inc=1, device_id={"chan": cross_chan, "split": 1 - s},
                device_id_type=pl.DeviceIdType.MESH,
            )
            pl.semaphore_wait(barrier, 1)

    adjoint_tables(W, B, row_taps, col_taps, gcols, gside, hrows)
    loads[0].wait()
    pl.semaphore_wait(barrier, C)

    def swap(to_a, has_a, to_b, has_b):
        @pl.when(has_a)
        def _():
            to_a.start()

        @pl.when(has_b)
        def _():
            to_b.start()

        def finish():
            @pl.when(has_a)
            def _():
                to_a.wait_send()
                to_b.wait_recv()

            @pl.when(has_b)
            def _():
                to_b.wait_send()
                to_a.wait_recv()

        return finish

    def clear(ref, lacking):
        @pl.when(jnp.logical_not(lacking))
        def _():
            ref[...] = jnp.zeros_like(ref)

    finish_u = swap(
        remote(u.at[:, :, pl.ds(R - PAD, PAD)], up, send_u.at[0], recv_u.at[0], down_id), has_down,
        remote(u.at[:, :, pl.ds(0, PAD)], lo, send_u.at[1], recv_u.at[1], up_id), has_up,
    )
    clear(up, has_up)
    clear(lo, has_down)
    has_left, has_right = mb > 0, mb < FC - 1
    side_half = per * MARGIN
    clear(spin.at[:, pl.ds(0, side_half)], has_left)
    clear(spin.at[:, pl.ds(side_half, side_half)], has_right)

    if groups == 1:
        spill_cols(R, 0, per, u, up, lo, gside, dcs, False)
        finish_u()
        spill_cols(R, 0, per, u, up, lo, gside, dcs, True)
        spill_rows(R, B, 0, hrows, dcs, spout)
    else:
        finish_u()

        @pl.loop(0, groups)
        def _(g):
            spill_cols(R, g, per, u, up, lo, gside, dcs, False)
            spill_cols(R, g, per, u, up, lo, gside, dcs, True)
            spill_rows(R, B, g, hrows, dcs, spout)

    finish_s = swap(
        remote(
            spout.at[:, pl.ds(0, side_half)], spin.at[:, pl.ds(side_half, side_half)],
            send_s.at[0], recv_s.at[0], left_id,
        ), has_left,
        remote(
            spout.at[:, pl.ds(side_half, side_half)], spin.at[:, pl.ds(0, side_half)],
            send_s.at[1], recv_s.at[1], right_id,
        ), has_right,
    )

    step = 256
    chunks = half // step

    def to_partner(buf, dst, lanes, i):
        return remote(buf.at[:, lanes], dst.at[:, lanes], send_p.at[i], recv_p.at[i], partner)

    def parts(j):
        return pl.ds(j * step, step), pl.ds(half + j * step, step)

    loads[1].wait()
    loads[2].wait()
    copies = []
    for j in range(chunks):
        for q, lanes in enumerate(parts(j)):
            half_chunk(FC, x, colT, hown, lanes)
            copy = to_partner(hown, hoth, lanes, 2 * j + q)
            copy.start()
            copies.append(copy)

    finish_s()
    for g in range(groups):
        sides[g] = spin[g].astype(f32).T.astype(bf16)

    def peer(i):
        return (me + C // 2 + (i + 1) // 2 * (1 - 2 * (i % 2))) % C

    def send_adjoint(i):
        return remote(
            adj.at[i], radj.at[me], send_a.at[i], recv_a.at[me], {"chan": peer(i), "split": s}
        )

    @pl.loop(0, groups)
    def _(g):
        for pair in range(0, per, 2):
            i = g * per + pair
            chans = (peer(i), peer(i + 1))

            def store(e, k, value):
                adj[i + e, k * B : k * B + B] = value

            adjoint_pair(R, W, B, chans, u, up, lo, gcols, hrows, sides, dc, store)
            send_adjoint(i).start()

            @pl.when(i + 1 < C - 1)
            def _():
                send_adjoint(i + 1).start()

            @pl.when(i + 1 == C - 1)
            def _():
                radj[me] = adj[C - 1]

    table_body(s, FR, R, colT, bown, aown, aoth)
    for copy in loads[3:]:
        copy.wait()
    second = []
    for j in range(chunks):
        copies[2 * j].wait()
        copies[2 * j + 1].wait()
        vis_chunk(aown, aoth, hown, hoth, wts, wown, *parts(j))
        for q, lanes in enumerate(parts(j)):
            copy = to_partner(wown, woth, lanes, 2 * chunks + 2 * j + q)
            copy.start()
            second.append(copy)
    forward_tables(W, B, row_taps, col_taps, fcols, frows)
    clear(ic.at[:, pl.ds(0, PAD)], has_up)
    clear(ic.at[:, pl.ds(PAD + R, PAD)], has_down)
    for j in range(chunks):
        second[2 * j].wait()
        second[2 * j + 1].wait()
        back_chunk(s, half, bown, wown, woth, back, *parts(j))
    gradient_body(FC, W, back, colT, x, d, pre)

    k = lax.broadcasted_iota(jnp.int32, (2 * MARGIN, W), 0)
    col = lax.broadcasted_iota(jnp.int32, (2 * MARGIN, W), 1)
    take_left = jnp.where((k < MARGIN) & (col == W - MARGIN + k), 1.0, 0.0)
    take_right = jnp.where((k >= MARGIN) & (col == k - MARGIN), 1.0, 0.0)

    def deliver(buf, dst, ssem, rsem, i, start):
        b = (mb + i) % FC
        for j in range(FR):
            f = b * FR + (ma + j) % FR
            r = i * FR + j
            if r == 0:
                if start:
                    dst[me] = buf[f]
                continue
            copy = remote(buf.at[f], dst.at[me], ssem.at[r], rsem.at[r], {"chan": f, "split": s})
            if start:
                copy.start()
            else:
                copy.wait_send()

    def image_cell(i):
        b = (mb + i) % FC
        for j in range(FR):
            if i or j:
                f = b * FR + (ma + j) % FR
                remote(adj.at[0], radj.at[f], send_a.at[0], recv_a.at[f], partner).wait_recv()
        lanes = pl.ds(pl.multiple_of(b * W, W), W)
        pieces = [radj[b * FR + a] for a in range(FR)]
        main = jnp.concatenate(pieces, axis=0) if FR > 1 else pieces[0]
        upd = pre[:, lanes] - primal_step * main.astype(f32)
        nb = jnp.maximum(upd, 0.0).astype(bf16)
        eb = (2.0 * nb.astype(f32) - x[b].astype(f32)).astype(bf16)
        new[b] = nb
        for a in range(FR):
            ext[b * FR + a] = eb[a * R : (a + 1) * R]
        deliver(ext, rmain, send_e, recv_e, i, True)

    def image_sides(i):
        b = (mb + i) % FC
        left = jnp.where(b > 0, take_left, 0.0).astype(bf16)
        right = jnp.where(b < FC - 1, take_right, 0.0).astype(bf16)
        nt = (((1,), (1,)), ((), ()))
        for a in range(FR):
            lf = (b + FC - 1) % FC * FR + a
            rf = (b + 1) % FC * FR + a
            both = lax.dot_general(left, ext[lf], nt, preferred_element_type=f32)
            both = both + lax.dot_general(right, ext[rf], nt, preferred_element_type=f32)
            exts[b * FR + a] = both.astype(bf16)
        deliver(exts, rsides, send_es, recv_es, i, True)

    order = [0] + [FC // 2 - (i + 1) // 2 * (1 - 2 * (i % 2)) for i in range(FC - 1)]
    ready, sided = set(), []
    for i in order:
        image_cell(i)
        ready.add(i)
        for q in order:
            if q not in sided and {(q + 1) % FC, (q - 1) % FC} <= ready:
                image_sides(q)
                sided.append(q)

    def halo(c, i):
        lanes = pl.ds(pl.multiple_of(c * W, W), W)
        return swap(
            remote(
                ic.at[:, pl.ds(R, PAD), lanes], ic.at[:, pl.ds(0, PAD), lanes],
                send_h.at[i], recv_h.at[c], down_id,
            ), has_down,
            remote(
                ic.at[:, pl.ds(PAD, PAD), lanes], ic.at[:, pl.ds(PAD + R, PAD), lanes],
                send_h.at[C + i], recv_h.at[C + c], up_id,
            ), has_up,
        )

    pending = []
    started = []

    def rows_of(count):
        batch = pending[:count]
        del pending[:count]
        for _, finish in batch:
            finish()
        forward_rows(R, W, B, [c for c, _ in batch], not started, ic, frows, u, total)
        started.append(True)

    for i in sided:
        for j in range(FR):
            r = i * FR + j
            src_b, src_a = (mb + FC - i) % FC, (ma + FR - j) % FR
            c = src_b * FR + src_a
            if r:
                device = {"chan": c, "split": s}
                remote(exts.at[c], rsides.at[c], send_es.at[r], recv_es.at[r], device).wait_recv()
                remote(ext.at[c], rmain.at[c], send_e.at[r], recv_e.at[r], device).wait_recv()
            forward_cols(R, W, c, rmain, rsides, fcols, ic)
            pending.append((c, halo(c, r)))
            if FR == 1 and len(pending) == 4:
                rows_of(2)
    while pending:
        rows_of(2)

    for i in range(FC):
        deliver(exts, rsides, send_es, recv_es, i, False)
        deliver(ext, rmain, send_e, recv_e, i, False)

    @pl.loop(0, C - 1)
    def _(i):
        send_adjoint(i).wait_send()


def per_device(sky_image, dirty_image, uv_weights, dual_coeffs, support_mask, row_taps, col_taps):
    FC, FR = sky_image.shape[1], sky_image.shape[2]
    R, W = sky_image.shape[4], sky_image.shape[5]
    C = dual_coeffs.shape[1]
    npix = FC * W
    half = npix // 2
    B = min(128, R)
    RP = R + 2 * PAD
    per = W // (2 * MARGIN)
    u = dual_coeffs.reshape(NB, C, R, W)
    x = sky_image.reshape(FC, FR * R, W)
    d = dirty_image.reshape(FC, FR * R, W)
    wts = uv_weights.reshape(half, half)
    mask = support_mask.reshape(R, W)
    colT = col_dft(npix)
    vm = lambda *shape: pltpu.VMEM(shape, bf16)
    sem = lambda n: pltpu.SemaphoreType.DMA((n,))
    any_spec = pl.BlockSpec(memory_space=pl.ANY)
    smem_spec = pl.BlockSpec(memory_space=pltpu.SMEM)
    vmem_spec = pl.BlockSpec(memory_space=pltpu.VMEM)
    span = B + 2 * PAD
    held = pl.pallas_call(
        functools.partial(step_kernel, C, FC, FR, R, W, B),
        out_shape=[
            vm(FC, FR * R, W), vm(NB, C, R, W), pltpu.VMEM((NB, R, W), f32),
            pltpu.VMEM((R, W), jnp.int32),
        ],
        in_specs=[any_spec] * 6 + [smem_spec] * 2,
        out_specs=[vmem_spec] * 4,
        scratch_shapes=[
            vm(FC, FR * R, W), vm(FC, FR * R, W), pltpu.VMEM((half, half), jnp.int32), vm(npix, npix),
            vm(NB, 2 * W, 2 * W), vm(NB, per * W, W), vm(B, NB * span), vm(W + 16, NB * W), vm(NB, B, span),
            vm(NB, C, PAD, W), vm(NB, C, PAD, W), vm(NB, RP, 2 * W), vm(NB, RP, W),
            vm(C // per, W, R), vm(C // per, W, R), vm(C // per, R, W), vm(C, R, W), vm(C, R, W),
            *[vm(half, npix)] * 8, pltpu.VMEM((half, npix), f32),
            vm(C, R, W), vm(C, 16, R), vm(C, R, W), vm(C, 16, R), vm(NB, RP, C * W),
            sem(2), sem(2), sem(2), sem(2), sem(C), sem(C),
            sem(C), sem(C), sem(C), sem(C), sem(4 * half // 128), sem(4 * half // 128),
            sem(2 * C), sem(2 * C), sem(6),
        ],
        compiler_params=pltpu.CompilerParams(
            collective_id=0, has_side_effects=True, vmem_limit_bytes=50 * 2**20
        ),
    )(u, x, d, wts, mask, colT, row_taps, col_taps)
    new, steps, total, mask = [pltpu.with_memory_space_constraint(a, pltpu.VMEM) for a in held]

    new_dual, new = pl.pallas_call(
        functools.partial(shrink_body, C, R, W, B),
        in_specs=[vmem_spec] * 4,
        out_specs=[any_spec] * 2,
        out_shape=[
            jax.ShapeDtypeStruct((NB, C, R, W), bf16),
            jax.ShapeDtypeStruct((FC, FR * R, W), bf16),
        ],
        scratch_shapes=[vm(NB, C, R, W), pltpu.SemaphoreType.DMA, sem(NB)],
        compiler_params=pltpu.CompilerParams(vmem_limit_bytes=50 * 2**20),
    )(steps, total, mask, new)
    return (new.reshape(sky_image.shape), new_dual.reshape(dual_coeffs.shape))


def solution(mesh):
    placed = (
        P(("cube", "chan"), None, None, "split", None, None),
        P(("cube", "chan"), None, None, "split", None, None),
        P(("cube", "chan"), "split", None),
        P(None, "cube", "chan", "split", None, None),
        P("chan", "split", None, None),
        P(),
        P(),
    )
    return jax.shard_map(
        per_device,
        mesh=mesh,
        in_specs=placed,
        out_specs=(
            P(("cube", "chan"), None, None, "split", None, None),
            P(None, "cube", "chan", "split", None, None),
        ),
        check_vma=False,
    )
```

```python
import functools
import math

import jax
import jax.numpy as jnp
import numpy as np
from jax import lax
from jax.experimental import pallas as pl
from jax.experimental.pallas import tpu as pltpu
from jax.sharding import PartitionSpec as P

NB = 4
TAPS = 17
MARGIN = 8
PAD = 16
LAG = 2

primal_step = 0.5
dual_step = 0.5
radius = 6.0
weight_unit = 0.25
f32 = jnp.float32
bf16 = jnp.bfloat16


def dot(a, b):
    return jnp.dot(a, b, preferred_element_type=f32)


def col_dft(npix):
    half = npix // 2
    product = np.arange(npix)[:, None] * np.arange(half)[None, :] % npix
    phases = product.astype(np.float32) * np.float32(2.0 * math.pi / npix)
    factor = np.float32(1.0 / math.sqrt(npix))
    table = np.concatenate([np.cos(phases) * factor, -np.sin(phases) * factor], axis=1)
    return jnp.asarray(table.astype(jnp.bfloat16))


def bands(index, taps):
    outs = [jnp.zeros(index.shape, f32) for _ in range(NB)]
    for t in range(TAPS):
        hit = index == t
        outs = [jnp.where(hit, taps[n, t], outs[n]) for n in range(NB)]
    return [o.astype(bf16) for o in outs]


def adjoint_tables(W, B, row_taps, col_taps, gcols, hrows):
    span = B + 2 * PAD
    i = lax.broadcasted_iota(jnp.int32, (W, W), 0)
    j = lax.broadcasted_iota(jnp.int32, (W, W), 1)
    main_bands = bands(j - i + MARGIN, col_taps)
    for n in range(NB):
        none = jnp.zeros((W, W), bf16)
        gcols[n, :W, :W] = main_bands[n]
        gcols[n, :W, W:] = none
        gcols[n, W:, :W] = none
        gcols[n, W:, W:] = main_bands[n]
    r = lax.broadcasted_iota(jnp.int32, (B, NB * span), 0)
    w = lax.broadcasted_iota(jnp.int32, (B, NB * span), 1)
    basis = lax.broadcasted_iota(jnp.int32, (1, NB * span), 1) // span
    index = r - w % span + PAD + MARGIN
    out = jnp.zeros(index.shape, f32)
    for t in range(TAPS):
        tap = jnp.full(basis.shape, row_taps[0, t], f32)
        for n in range(1, NB):
            tap = jnp.where(basis == n, row_taps[n, t], tap)
        out = jnp.where(index == t, tap, out)
    hrows[...] = out.astype(bf16)


def side_tables(W, col_taps, gside):
    per = W // (2 * MARGIN)
    i = lax.broadcasted_iota(jnp.int32, (W, W), 0)
    j = lax.broadcasted_iota(jnp.int32, (W, W), 1)
    jj = j % (W // 2)
    side = jnp.where(j < W // 2, jj - MARGIN, W + jj)
    side_bands = bands(jnp.where(jj < MARGIN, side - i + MARGIN, -1), col_taps)
    for n in range(NB):
        table = side_bands[n].astype(f32)
        for cc in range(per):
            moved = pltpu.roll(table, cc * MARGIN, 1) if cc else table
            gside[n, cc * W : (cc + 1) * W] = moved.astype(bf16)


def forward_tables(W, B, row_taps, col_taps, fcols, frows):
    i = lax.broadcasted_iota(jnp.int32, (W, W), 0)
    j = lax.broadcasted_iota(jnp.int32, (W, W), 1)
    main_bands = bands(i - j + MARGIN, col_taps)
    k = lax.broadcasted_iota(jnp.int32, (2 * MARGIN, W), 0)
    jk = lax.broadcasted_iota(jnp.int32, (2 * MARGIN, W), 1)
    side = jnp.where(k < MARGIN, k - MARGIN, W - MARGIN + k)
    side_bands = bands(side - jk + MARGIN, col_taps)
    r = lax.broadcasted_iota(jnp.int32, (B, B + 2 * PAD), 0)
    w = lax.broadcasted_iota(jnp.int32, (B, B + 2 * PAD), 1)
    row_bands = bands(w - r - PAD + MARGIN, row_taps)
    for n in range(NB):
        fcols[:W, n * W : (n + 1) * W] = main_bands[n]
        fcols[W:, n * W : (n + 1) * W] = side_bands[n]
        frows[n] = row_bands[n]


def spill_cols(R, group, per, u, up, lo, gside, dcs, halo):
    for n in range(NB):
        table = gside[n]
        if halo:
            top = jnp.concatenate([up[n, group * per + cc] for cc in range(per)], axis=1)
            bottom = jnp.concatenate([lo[n, group * per + cc] for cc in range(per)], axis=1)
            out = dot(jnp.concatenate([top, bottom], axis=0), table).astype(bf16)
            dcs[n, :PAD] = out[:PAD]
            dcs[n, PAD + R :] = out[PAD:]
        else:
            rows = jnp.concatenate([u[n, group * per + cc] for cc in range(per)], axis=1)
            dcs[n, PAD : PAD + R] = dot(rows, table).astype(bf16)


def stack_rows(buf, k, B):
    span = B + 2 * PAD
    return jnp.concatenate([buf[n, k * B : k * B + span] for n in range(NB)], axis=0)


def spill_rows(R, B, group, hrows, dcs, spout):
    for k in range(R // B):
        spout[group, :, k * B : k * B + B] = dot(hrows[...], stack_rows(dcs, k, B)).T.astype(bf16)


def place_sides(W, cc):
    row = lax.broadcasted_iota(jnp.int32, (W, W), 0)
    col = lax.broadcasted_iota(jnp.int32, (W, W), 1)
    rr = row % (W // 2)
    target = jnp.where(row < W // 2, 0, W - MARGIN) + rr % MARGIN
    return jnp.where((rr // MARGIN == cc) & (col == target), 1.0, 0.0).astype(bf16)


def pick_sides(W, cc):
    row = lax.broadcasted_iota(jnp.int32, (2 * MARGIN, W), 0)
    col = lax.broadcasted_iota(jnp.int32, (2 * MARGIN, W), 1)
    source = jnp.where(row < MARGIN, 0, W // 2 - MARGIN) + cc * MARGIN + row
    return jnp.where(col == source, 1.0, 0.0).astype(bf16)


def first_pair_cols(R, chans, u, gcols, dc):
    for n in range(NB):
        dc[n, PAD : PAD + R] = dot(
            jnp.concatenate([u[n, c] for c in chans], axis=1), gcols[n]
        ).astype(bf16)
        dc[n, :PAD] = jnp.zeros_like(dc[n, :PAD])
        dc[n, PAD + R :] = jnp.zeros_like(dc[n, PAD + R :])


def first_pair_halo(R, chans, up, lo, gcols, dc):
    for n in range(NB):
        top = jnp.concatenate([up[n, c] for c in chans], axis=1)
        bottom = jnp.concatenate([lo[n, c] for c in chans], axis=1)
        out = dot(jnp.concatenate([top, bottom], axis=0), gcols[n]).astype(bf16)
        dc[n, :PAD] = out[:PAD]
        dc[n, PAD + R :] = out[PAD:]


def first_pair_rows(W, B, k, hrows, dc, adj):
    start = pl.multiple_of(k * B, B)
    block = [dc[n, pl.ds(start, B + 2 * PAD)] for n in range(NB)]
    out = dot(hrows[...], jnp.concatenate(block, axis=0)).astype(bf16)
    for e in range(2):
        adj[e, pl.ds(start, B)] = out[:, e * W : (e + 1) * W]


def adjoint_pair(R, W, B, chans, u, up, lo, gcols, hrows, sides, dc, store):
    per = W // (2 * MARGIN)
    for n in range(NB):
        rows = [jnp.concatenate([up[n, c], u[n, c], lo[n, c]], axis=0) for c in chans]
        dc[n] = dot(jnp.concatenate(rows, axis=1), gcols[n]).astype(bf16)
    place = [place_sides(W, c % per) for c in chans]
    for k in range(R // B):
        out = dot(hrows[...], stack_rows(dc, k, B))
        for e, c in enumerate(chans):
            moved = dot(sides[c // per, k * B : k * B + B], place[e])
            store(e, k, (out[:, e * W : (e + 1) * W] + moved).astype(bf16))


def half_chunk(FC, x, colT, out, lanes):
    rows = jnp.concatenate([x[b] for b in range(FC)], axis=1)
    out[:, lanes] = dot(rows, colT[:, lanes]).astype(bf16)


def table_body(s, FR, R, colT, bown, aown, aoth):
    half = FR * R
    for a in range(FR):
        own = pl.ds(pl.multiple_of((2 * a + s) * R, R), R)
        bown[a * R : (a + 1) * R] = colT[own, :]
    odd_lane = lax.broadcasted_iota(jnp.int32, (1, half), 1) % 2 == 1
    flip = jnp.where(odd_lane & (s == 1), -1.0, 1.0).astype(f32)
    odd_row = lax.broadcasted_iota(jnp.int32, (half, 1), 0) % 2 == 1
    for dst, part in ((aown, s), (aoth, 1 - s)):
        for q in range(2):
            lanes = slice(q * half, (q + 1) * half)
            if FR == 1:
                sign = jnp.where(odd_row & (part == 1), -1.0, 1.0).astype(f32)
                dst[:, lanes] = (colT[:half, lanes].astype(f32) * (sign * flip)).astype(bf16)
                continue
            pieces = [
                colT[pl.ds(pl.multiple_of((2 * a + part) * R, R), R), lanes] for a in range(FR)
            ]
            block = jnp.concatenate(pieces, axis=0)
            dst[:, lanes] = (block.astype(f32).T * flip).astype(bf16)


def stack_re_im(ref, lanes_re, lanes_im, transpose):
    re, im = ref[:, lanes_re], ref[:, lanes_im]
    if transpose:
        return jnp.concatenate([re, im], 0), jnp.concatenate([im, -re], 0)
    return jnp.concatenate([re, -im], 0), jnp.concatenate([im, re], 0)


def vis_chunk(aown, aoth, hown, hoth, wts, out, re_l, im_l):
    own_re, own_im = stack_re_im(hown, re_l, im_l, False)
    oth_re, oth_im = stack_re_im(hoth, re_l, im_l, False)
    scale = weight_unit * wts[:, re_l].astype(f32)
    re = dot(aown[...], own_re) + dot(aoth[...], oth_re)
    out[:, re_l] = (scale * re).astype(bf16)
    im = dot(aown[...], own_im) + dot(aoth[...], oth_im)
    out[:, im_l] = (scale * im).astype(bf16)


def back_chunk(s, half, bown, wown, woth, out, re_l, im_l):
    odd = lax.broadcasted_iota(jnp.int32, (half, 1), 0) % 2 == 1
    own_sign = jnp.where(odd & (s == 1), -1.0, 1.0)
    oth_sign = jnp.where(odd & (s == 0), -1.0, 1.0)
    own_re, own_im = stack_re_im(wown, re_l, im_l, True)
    oth_re, oth_im = stack_re_im(woth, re_l, im_l, True)
    re = own_sign * dot(bown[...], own_re) + oth_sign * dot(bown[...], oth_re)
    out[:, re_l] = re.astype(bf16)
    im = own_sign * dot(bown[...], own_im) + oth_sign * dot(bown[...], oth_im)
    out[:, im_l] = im.astype(bf16)


def gradient_body(FC, W, back, colT, x, d, pre):
    step = 2 * W

    @pl.loop(0, FC // 2)
    def _(j):
        lanes = pl.ds(pl.multiple_of(j * step, step), step)
        grad = lax.dot_general(
            back[...], colT[lanes, :], (((1,), (1,)), ((), ())), preferred_element_type=f32
        )
        xs = jnp.concatenate([x[2 * j], x[2 * j + 1]], axis=1).astype(f32)
        ds = jnp.concatenate([d[2 * j], d[2 * j + 1]], axis=1).astype(f32)
        pre[:, lanes] = xs - primal_step * (grad - ds)


def forward_cols(R, W, c, block, fcols, ic):
    cut = min(R, W)
    sides = [block[c, R + at * PAD : R + at * PAD + PAD, :cut] for at in range(R // cut)]
    sides = jnp.concatenate(sides, axis=1) if len(sides) > 1 else sides[0]
    rows = jnp.concatenate([block[c, :R], sides.astype(f32).T.astype(bf16)], axis=1)
    out = dot(rows, fcols[...])
    lanes = pl.ds(pl.multiple_of(c * W, W), W)
    for n in range(NB):
        ic[n, PAD : PAD + R, lanes] = out[:, n * W : (n + 1) * W].astype(bf16)


def forward_rows(R, W, B, chans, first, ic, frows, u, total):
    span = B + 2 * PAD
    lanes = [pl.ds(pl.multiple_of(c * W, W), W) for c in chans]
    for n in range(NB):
        for k in range(R // B):
            rows = slice(k * B, (k + 1) * B)
            block = [ic[n, k * B : k * B + span, at] for at in lanes]
            coef = dot(frows[n], jnp.concatenate(block, axis=1) if len(block) > 1 else block[0])
            acc = None if first else total[n, rows]
            for e, c in enumerate(chans):
                st = u[n, c, rows].astype(f32) + dual_step * coef[:, e * W : (e + 1) * W]
                u[n, c, rows] = st.astype(bf16)
                acc = st * st if acc is None else acc + st * st
            total[n, rows] = acc


def shrink_body(C, R, W, B, st, total, mask, new_in, out_hbm, new_hbm, out, sem_new, sem):
    moved = pltpu.make_async_copy(new_in, new_hbm, sem_new)
    moved.start()
    copies = []
    for n in range(NB):
        for k in range(R // B):
            rows = slice(k * B, (k + 1) * B)
            keep = radius * mask[rows].astype(f32)
            scale = keep / jnp.maximum(jnp.sqrt(total[n, rows]), radius)
            for c in range(C):
                out[n, c, rows] = (st[n, c, rows].astype(f32) * scale).astype(bf16)
        copy = pltpu.make_async_copy(out.at[n], out_hbm.at[n], sem.at[n])
        copy.start()
        copies.append(copy)
    for copy in copies:
        copy.wait()
    moved.wait()


def step_kernel(
    C, FC, FR, R, W, B,
    u_hbm, x_hbm, d_hbm, wts_hbm, mask_hbm, colT_hbm, row_taps, col_taps,
    new, u, total, mask,
    x, d, wts, colT, gcols, gside, hrows, fcols, frows,
    up, lo, dc, dcs, spout, spin, sides, adj, radj, fix, rfix,
    hown, hoth, wown, woth, back, bown, aown, aoth, pre,
    ext, rmain, ic,
    send_u, recv_u, send_s, recv_s, send_a, recv_a, send_b, recv_b, send_f, recv_f,
    send_e, recv_e, send_p, recv_p, send_h, recv_h, load, load_u,
):
    half = FC * W // 2
    me = lax.axis_index("chan")
    s = lax.axis_index("split")
    ma, mb = me % FR, me // FR
    has_up = (ma > 0) | (s == 1)
    has_down = (ma < FR - 1) | (s == 0)
    partner = {"chan": me, "split": 1 - s}
    down_id = {"chan": (me + s) % C, "split": 1 - s}
    up_id = {"chan": (me + s + C - 1) % C, "split": 1 - s}
    left_id = {"chan": (me + C - FR) % C, "split": s}
    right_id = {"chan": (me + FR) % C, "split": s}
    per = W // (2 * MARGIN)
    groups = C // per
    early = FR == 1 and R > B

    def remote(src, dst, ssem, rsem, device):
        return pltpu.make_async_remote_copy(
            src_ref=src, dst_ref=dst, send_sem=ssem, recv_sem=rsem,
            device_id=device, device_id_type=pl.DeviceIdType.MESH,
        )

    loads = [
        pltpu.make_async_copy(a, b, load.at[i])
        for i, (a, b) in enumerate(
            [(x_hbm, x), (colT_hbm, colT), (wts_hbm, wts), (d_hbm, d), (mask_hbm, mask)]
        )
    ]

    def peer(i):
        return (me + C // 2 + (i + 1) // 2 * (1 - 2 * (i % 2))) % C

    def load_duals(i):
        c = peer(i)
        return pltpu.make_async_copy(u_hbm.at[:, c], u.at[:, c], load_u.at[i])

    @pl.loop(0, C)
    def _(i):
        load_duals(i).start()

    for copy in loads:
        copy.start()
    barrier = pltpu.get_barrier_semaphore()

    @pl.loop(1, C)
    def _(i):
        pl.semaphore_signal(
            barrier, inc=1, device_id={"chan": (me + i) % C, "split": s},
            device_id_type=pl.DeviceIdType.MESH,
        )

    pl.semaphore_signal(barrier, inc=1, device_id=partner, device_id_type=pl.DeviceIdType.MESH)
    if FR > 1:
        cross = jnp.where(s == 0, ma > 0, ma < FR - 1)
        cross_chan = jnp.where(s == 0, (me + C - 1) % C, (me + 1) % C)

        @pl.when(cross)
        def _():
            pl.semaphore_signal(
                barrier, inc=1, device_id={"chan": cross_chan, "split": 1 - s},
                device_id_type=pl.DeviceIdType.MESH,
            )
            pl.semaphore_wait(barrier, 1)

    adjoint_tables(W, B, row_taps, col_taps, gcols, hrows)
    def swap(to_a, has_a, to_b, has_b):
        @pl.when(has_a)
        def _():
            to_a.start()

        @pl.when(has_b)
        def _():
            to_b.start()

        def finish():
            @pl.when(has_a)
            def _():
                to_a.wait_send()
                to_b.wait_recv()

            @pl.when(has_b)
            def _():
                to_b.wait_send()
                to_a.wait_recv()

        return finish

    def clear(ref, lacking):
        @pl.when(jnp.logical_not(lacking))
        def _():
            ref[...] = jnp.zeros_like(ref)

    clear(up, has_up)
    clear(lo, has_down)
    has_left, has_right = mb > 0, mb < FC - 1
    side_half = per * MARGIN
    clear(spin.at[:, pl.ds(0, side_half)], has_left)
    clear(spin.at[:, pl.ds(side_half, side_half)], has_right)

    def send_adjoint(i):
        return remote(
            adj.at[i], radj.at[me], send_a.at[i], recv_a.at[me], {"chan": peer(i), "split": s}
        )

    inner = pl.ds(pl.multiple_of(s * B, B), R - B)
    outer = pl.ds(pl.multiple_of((1 - s) * (R - B), B), B)

    def send_inner(i):
        return remote(
            adj.at[i, inner], radj.at[me, inner], send_a.at[i], recv_a.at[me],
            {"chan": peer(i), "split": s},
        )

    def send_outer(i):
        return remote(
            adj.at[i, outer], radj.at[me, outer], send_b.at[i], recv_b.at[i],
            {"chan": peer(i), "split": s},
        )

    def send_fix(i):
        return remote(
            fix.at[i], rfix.at[i], send_f.at[i], recv_f.at[i], {"chan": peer(i), "split": s}
        )

    def halo_duals(at, i):
        return swap(
            remote(
                u.at[:, at, pl.ds(R - PAD, PAD)], up.at[:, at], send_u.at[i], recv_u.at[i], down_id
            ), has_down,
            remote(
                u.at[:, at, pl.ds(0, PAD)], lo.at[:, at], send_u.at[C + i], recv_u.at[C + i], up_id
            ), has_up,
        )

    if early:
        firsts = (peer(0), peer(1))
        load_duals(0).wait()
        load_duals(1).wait()
        first_pair_cols(R, firsts, u, gcols, dc)
        last = R // B - 1
        for k in range(last):
            first_pair_rows(W, B, k + s, hrows, dc, adj)
        pl.semaphore_wait(barrier, C)
        send_inner(0).start()
        send_inner(1).start()
        side_tables(W, col_taps, gside)
        halos = [halo_duals(firsts[i], i) for i in range(2)]
        for i in range(2, C):
            load_duals(i).wait()
            halos.append(halo_duals(peer(i), i))
        for g in range(groups):
            spill_cols(R, g, per, u, up, lo, gside, dcs.at[g], False)
        for finish in halos[:2]:
            finish()
        first_pair_halo(R, firsts, up, lo, gcols, dc)
        first_pair_rows(W, B, last * (1 - s), hrows, dc, adj)
        send_outer(0).start()
        send_outer(1).start()
        for finish in halos[2:]:
            finish()
        for g in range(groups):
            spill_cols(R, g, per, u, up, lo, gside, dcs.at[g], True)
            spill_rows(R, B, g, hrows, dcs.at[g], spout)
    else:
        side_tables(W, col_taps, gside)

        @pl.loop(0, C)
        def _(i):
            load_duals(i).wait()

        pl.semaphore_wait(barrier, C)
        halo_duals(slice(None), 0)()

        @pl.loop(0, groups)
        def _(g):
            spill_cols(R, g, per, u, up, lo, gside, dcs.at[0], False)
            spill_cols(R, g, per, u, up, lo, gside, dcs.at[0], True)
            spill_rows(R, B, g, hrows, dcs.at[0], spout)

    finish_s = swap(
        remote(
            spout.at[:, pl.ds(0, side_half)], spin.at[:, pl.ds(side_half, side_half)],
            send_s.at[0], recv_s.at[0], left_id,
        ), has_left,
        remote(
            spout.at[:, pl.ds(side_half, side_half)], spin.at[:, pl.ds(0, side_half)],
            send_s.at[1], recv_s.at[1], right_id,
        ), has_right,
    )

    step = 256
    chunks = half // step

    def to_partner(buf, dst, lanes, i):
        return remote(buf.at[:, lanes], dst.at[:, lanes], send_p.at[i], recv_p.at[i], partner)

    def parts(j):
        return pl.ds(j * step, step), pl.ds(half + j * step, step)

    loads[0].wait()
    loads[1].wait()
    copies = []
    for j in range(chunks):
        for q, lanes in enumerate(parts(j)):
            half_chunk(FC, x, colT, hown, lanes)
            copy = to_partner(hown, hoth, lanes, 2 * j + q)
            copy.start()
            copies.append(copy)

    finish_s()
    for g in range(groups):
        sides[g] = spin[g].astype(f32).T.astype(bf16)

    def adjoint_step(i):
        chans = (peer(i), peer(i + 1))

        def store(e, k, value):
            adj[i + e, k * B : k * B + B] = value

        adjoint_pair(R, W, B, chans, u, up, lo, gcols, hrows, sides, dc, store)
        send_adjoint(i).start()

        @pl.when(i + 1 < C - 1)
        def _():
            send_adjoint(i + 1).start()

        @pl.when(i + 1 == C - 1)
        def _():
            radj[me] = adj[C - 1]

    if early:
        for i, c in enumerate(firsts):
            fix[i] = dot(pick_sides(W, c % per), spin[c // per]).astype(bf16)
            send_fix(i).start()
        for i in range(2, C, 2):
            adjoint_step(i)
    else:
        @pl.loop(0, groups)
        def _(g):
            for pair in range(0, per, 2):
                adjoint_step(g * per + pair)

    table_body(s, FR, R, colT, bown, aown, aoth)
    for copy in loads[2:]:
        copy.wait()
    second = []
    for j in range(chunks):
        copies[2 * j].wait()
        copies[2 * j + 1].wait()
        vis_chunk(aown, aoth, hown, hoth, wts, wown, *parts(j))
        for q, lanes in enumerate(parts(j)):
            copy = to_partner(wown, woth, lanes, 2 * chunks + 2 * j + q)
            copy.start()
            second.append(copy)
    forward_tables(W, B, row_taps, col_taps, fcols, frows)
    clear(ic.at[:, pl.ds(0, PAD)], has_up)
    clear(ic.at[:, pl.ds(PAD + R, PAD)], has_down)
    for j in range(chunks):
        second[2 * j].wait()
        second[2 * j + 1].wait()
        back_chunk(s, half, bown, wown, woth, back, *parts(j))
    gradient_body(FC, W, back, colT, x, d, pre)

    k = lax.broadcasted_iota(jnp.int32, (2 * MARGIN, W), 0)
    col = lax.broadcasted_iota(jnp.int32, (2 * MARGIN, W), 1)
    take_left = jnp.where((k < MARGIN) & (col == W - MARGIN + k), 1.0, 0.0)
    put_back = jnp.where(col == jnp.where(k < MARGIN, k, W - 2 * MARGIN + k), 1.0, 0.0).astype(bf16)
    take_right = jnp.where((k >= MARGIN) & (col == k - MARGIN), 1.0, 0.0)

    def deliver(i, start):
        b = (mb + i) % FC
        for j in range(FR):
            f = b * FR + (ma + j) % FR
            r = i * FR + j
            if r == 0:
                if start:
                    rmain[me] = ext[f]
                continue
            copy = remote(
                ext.at[f], rmain.at[me], send_e.at[r], recv_e.at[r], {"chan": f, "split": s}
            )
            if start:
                copy.start()
            else:
                copy.wait_send()

    def image_cell(i):
        b = (mb + i) % FC
        at = order.index(i) - 1
        fixed = early and 0 <= at < 2
        for j in range(FR):
            if i or j:
                f = b * FR + (ma + j) % FR
                rows = inner if fixed else slice(None)
                remote(
                    adj.at[0, rows], radj.at[f, rows], send_a.at[0], recv_a.at[f], partner
                ).wait_recv()
        if fixed:
            send_outer(at).wait_recv()
            send_fix(at).wait_recv()
        lanes = pl.ds(pl.multiple_of(b * W, W), W)
        pieces = [radj[b * FR + a] for a in range(FR)]
        main = jnp.concatenate(pieces, axis=0) if FR > 1 else pieces[0]
        main = main.astype(f32)
        if fixed:
            main = main + lax.dot_general(
                rfix[at], put_back, (((0,), (0,)), ((), ())), preferred_element_type=f32
            )
        upd = pre[:, lanes] - primal_step * main
        nb = jnp.maximum(upd, 0.0).astype(bf16)
        eb = (2.0 * nb.astype(f32) - x[b].astype(f32)).astype(bf16)
        new[b] = nb
        for a in range(FR):
            ext[b * FR + a, :R] = eb[a * R : (a + 1) * R]

    cut = min(R, W)

    def image_sides(i):
        b = (mb + i) % FC
        left = jnp.where(b > 0, take_left, 0.0).astype(bf16)
        right = jnp.where(b < FC - 1, take_right, 0.0).astype(bf16)
        nt = (((1,), (1,)), ((), ()))
        for a in range(FR):
            lf = (b + FC - 1) % FC * FR + a
            rf = (b + 1) % FC * FR + a
            both = lax.dot_general(left, ext[lf, :R], nt, preferred_element_type=f32)
            both = both + lax.dot_general(right, ext[rf, :R], nt, preferred_element_type=f32)
            for at in range(R // cut):
                piece = both[:, at * cut : (at + 1) * cut].astype(bf16)
                ext[b * FR + a, R + at * PAD : R + at * PAD + PAD, :cut] = piece
        deliver(i, True)

    order = [0] + [FC // 2 - (i + 1) // 2 * (1 - 2 * (i % 2)) for i in range(FC - 1)]
    ready, sided = set(), []
    for i in order:
        image_cell(i)
        ready.add(i)
        for q in order:
            if q not in sided and {q, (q + 1) % FC, (q - 1) % FC} <= ready:
                image_sides(q)
                sided.append(q)

    def halo(c, i):
        lanes = pl.ds(pl.multiple_of(c * W, W), W)
        return swap(
            remote(
                ic.at[:, pl.ds(R, PAD), lanes], ic.at[:, pl.ds(0, PAD), lanes],
                send_h.at[i], recv_h.at[c], down_id,
            ), has_down,
            remote(
                ic.at[:, pl.ds(PAD, PAD), lanes], ic.at[:, pl.ds(PAD + R, PAD), lanes],
                send_h.at[C + i], recv_h.at[C + c], up_id,
            ), has_up,
        )

    sided.remove(0)
    arrivals = [(i, j) for i in [0] + sided for j in range(FR)]
    pending = []
    started = []

    def rows_of(count):
        batch = pending[:count]
        del pending[:count]
        for _, finish in batch:
            finish()
        forward_rows(R, W, B, [c for c, _ in batch], not started, ic, frows, u, total)
        started.append(True)

    for i, j in arrivals:
        r = i * FR + j
        src_b, src_a = (mb + FC - i) % FC, (ma + FR - j) % FR
        c = src_b * FR + src_a
        if r:
            device = {"chan": c, "split": s}
            remote(ext.at[c], rmain.at[c], send_e.at[r], recv_e.at[r], device).wait_recv()
        forward_cols(R, W, c, rmain, fcols, ic)
        pending.append((c, halo(c, r)))
        if FR == 1 and len(pending) > LAG:
            rows_of(1)
    while pending:
        rows_of(1 if FR == 1 else 2)

    for i in range(FC):
        deliver(i, False)

    if early:
        for i in range(2):
            send_inner(i).wait_send()
            send_outer(i).wait_send()
            send_fix(i).wait_send()

    @pl.loop(2 if early else 0, C - 1)
    def _(i):
        send_adjoint(i).wait_send()


def per_device(sky_image, dirty_image, uv_weights, dual_coeffs, support_mask, row_taps, col_taps):
    FC, FR = sky_image.shape[1], sky_image.shape[2]
    R, W = sky_image.shape[4], sky_image.shape[5]
    C = dual_coeffs.shape[1]
    npix = FC * W
    half = npix // 2
    B = min(128, R)
    RP = R + 2 * PAD
    per = W // (2 * MARGIN)
    u = dual_coeffs.reshape(NB, C, R, W)
    x = sky_image.reshape(FC, FR * R, W)
    d = dirty_image.reshape(FC, FR * R, W)
    wts = uv_weights.reshape(half, half)
    mask = support_mask.reshape(R, W)
    colT = col_dft(npix)
    vm = lambda *shape: pltpu.VMEM(shape, bf16)
    sem = lambda n: pltpu.SemaphoreType.DMA((n,))
    any_spec = pl.BlockSpec(memory_space=pl.ANY)
    smem_spec = pl.BlockSpec(memory_space=pltpu.SMEM)
    vmem_spec = pl.BlockSpec(memory_space=pltpu.VMEM)
    span = B + 2 * PAD
    extra = R // min(R, W) * PAD
    held = pl.pallas_call(
        functools.partial(step_kernel, C, FC, FR, R, W, B),
        out_shape=[
            vm(FC, FR * R, W), vm(NB, C, R, W), pltpu.VMEM((NB, R, W), f32),
            pltpu.VMEM((R, W), jnp.int32),
        ],
        in_specs=[any_spec] * 6 + [smem_spec] * 2,
        out_specs=[vmem_spec] * 4,
        scratch_shapes=[
            vm(FC, FR * R, W), vm(FC, FR * R, W), pltpu.VMEM((half, half), jnp.int32), vm(npix, npix),
            vm(NB, 2 * W, 2 * W), vm(NB, per * W, W), vm(B, NB * span), vm(W + 16, NB * W), vm(NB, B, span),
            vm(NB, C, PAD, W), vm(NB, C, PAD, W), vm(NB, RP, 2 * W),
            vm(C // per if FR == 1 else 1, NB, RP, W),
            vm(C // per, W, R), vm(C // per, W, R), vm(C // per, R, W), vm(C, R, W), vm(C, R, W),
            vm(2, 2 * MARGIN, R), vm(2, 2 * MARGIN, R),
            *[vm(half, npix)] * 8, pltpu.VMEM((half, npix), f32),
            vm(C, R + extra, W), vm(C, R + extra, W), vm(NB, RP, C * W),
            sem(2 * C), sem(2 * C), sem(2), sem(2), sem(C), sem(C), sem(2), sem(2), sem(2), sem(2),
            sem(C), sem(C), sem(4 * half // 128), sem(4 * half // 128),
            sem(2 * C), sem(2 * C), sem(5), sem(C),
        ],
        compiler_params=pltpu.CompilerParams(
            collective_id=0, has_side_effects=True, vmem_limit_bytes=50 * 2**20
        ),
    )(u, x, d, wts, mask, colT, row_taps, col_taps)
    new, steps, total, mask = [pltpu.with_memory_space_constraint(a, pltpu.VMEM) for a in held]

    new_dual, new = pl.pallas_call(
        functools.partial(shrink_body, C, R, W, B),
        in_specs=[vmem_spec] * 4,
        out_specs=[any_spec] * 2,
        out_shape=[
            jax.ShapeDtypeStruct((NB, C, R, W), bf16),
            jax.ShapeDtypeStruct((FC, FR * R, W), bf16),
        ],
        scratch_shapes=[vm(NB, C, R, W), pltpu.SemaphoreType.DMA, sem(NB)],
        compiler_params=pltpu.CompilerParams(vmem_limit_bytes=50 * 2**20),
    )(steps, total, mask, new)
    return (new.reshape(sky_image.shape), new_dual.reshape(dual_coeffs.shape))


def solution(mesh):
    placed = (
        P(("cube", "chan"), None, None, "split", None, None),
        P(("cube", "chan"), None, None, "split", None, None),
        P(("cube", "chan"), "split", None),
        P(None, "cube", "chan", "split", None, None),
        P("chan", "split", None, None),
        P(),
        P(),
    )
    return jax.shard_map(
        per_device,
        mesh=mesh,
        in_specs=placed,
        out_specs=(
            P(("cube", "chan"), None, None, "split", None, None),
            P(None, "cube", "chan", "split", None, None),
        ),
        check_vma=False,
    )
```

```python
import functools
import math

import jax
import jax.numpy as jnp
import numpy as np
from jax import lax
from jax.experimental import pallas as pl
from jax.experimental.pallas import tpu as pltpu
from jax.sharding import PartitionSpec as P

NB = 4
TAPS = 17
MARGIN = 8
PAD = 16
LAG = 1

primal_step = 0.5
dual_step = 0.5
radius = 6.0
weight_unit = 0.25
f32 = jnp.float32
bf16 = jnp.bfloat16


def dot(a, b):
    return jnp.dot(a, b, preferred_element_type=f32)


def col_dft(npix):
    half = npix // 2
    product = np.arange(npix)[:, None] * np.arange(half)[None, :] % npix
    phases = product.astype(np.float32) * np.float32(2.0 * math.pi / npix)
    factor = np.float32(1.0 / math.sqrt(npix))
    table = np.concatenate([np.cos(phases) * factor, -np.sin(phases) * factor], axis=1)
    return jnp.asarray(table.astype(jnp.bfloat16))


def bands(index, taps):
    outs = [jnp.zeros(index.shape, f32) for _ in range(NB)]
    for t in range(TAPS):
        hit = index == t
        outs = [jnp.where(hit, taps[n, t], outs[n]) for n in range(NB)]
    return [o.astype(bf16) for o in outs]


def shifted_rows(rows, width, taps, n, lane_of):
    lane = lax.broadcasted_iota(jnp.int32, (8, width), 1)
    row = lax.broadcasted_iota(jnp.int32, (8, width), 0)
    place = (lane - row + width) % width
    base = jnp.zeros((8, width), f32)
    for t in range(TAPS):
        base = jnp.where(place == lane_of(t) % width, taps[n, t], base)
    blocks = [pltpu.roll(base, 8 * i, 1) if i else base for i in range(rows // 8)]
    return jnp.concatenate(blocks, axis=0)


def adjoint_tables(W, B, row_taps, col_taps, gcols, gside, hrows):
    span = B + 2 * PAD
    lane = lax.broadcasted_iota(jnp.int32, (W, W), 1)
    rows = []
    for n in range(NB):
        none = jnp.zeros((W, W), bf16)
        table = shifted_rows(W, 2 * W, col_taps, n, lambda t: t - MARGIN)
        main = table[:, :W].astype(bf16)
        gcols[n, :W, :W] = main
        gcols[n, :W, W:] = none
        gcols[n, W:, :W] = none
        gcols[n, W:, W:] = main
        out = table[:, W:]
        right = pltpu.roll(jnp.where(lane < MARGIN, out, 0.0), W // 2, 1)
        left = pltpu.roll(jnp.where(lane >= W - MARGIN, out, 0.0), MARGIN, 1)
        gside[n, :W] = (left + right).astype(bf16)
        rows.append(shifted_rows(B, 2 * W, row_taps, n, lambda t: PAD + MARGIN - t)[:, :span])
    hrows[...] = jnp.concatenate(rows, axis=1).astype(bf16)


def side_tables(W, gside):
    for n in range(NB):
        table = gside[n, :W].astype(f32)
        for cc in range(1, W // (2 * MARGIN)):
            gside[n, cc * W : (cc + 1) * W] = pltpu.roll(table, cc * MARGIN, 1).astype(bf16)


def forward_tables(W, B, row_taps, col_taps, fcols, frows):
    i = lax.broadcasted_iota(jnp.int32, (W, W), 0)
    j = lax.broadcasted_iota(jnp.int32, (W, W), 1)
    main_bands = bands(i - j + MARGIN, col_taps)
    k = lax.broadcasted_iota(jnp.int32, (2 * MARGIN, W), 0)
    jk = lax.broadcasted_iota(jnp.int32, (2 * MARGIN, W), 1)
    side = jnp.where(k < MARGIN, k - MARGIN, W - MARGIN + k)
    side_bands = bands(side - jk + MARGIN, col_taps)
    r = lax.broadcasted_iota(jnp.int32, (B, B + 2 * PAD), 0)
    w = lax.broadcasted_iota(jnp.int32, (B, B + 2 * PAD), 1)
    row_bands = bands(w - r - PAD + MARGIN, row_taps)
    for n in range(NB):
        fcols[:W, n * W : (n + 1) * W] = main_bands[n]
        fcols[W:, n * W : (n + 1) * W] = side_bands[n]
        frows[n] = row_bands[n]


def spill_cols(R, group, per, u, up, lo, gside, dcs, halo):
    for n in range(NB):
        table = gside[n]
        if halo:
            top = jnp.concatenate([up[n, group * per + cc] for cc in range(per)], axis=1)
            bottom = jnp.concatenate([lo[n, group * per + cc] for cc in range(per)], axis=1)
            out = dot(jnp.concatenate([top, bottom], axis=0), table).astype(bf16)
            dcs[n, :PAD] = out[:PAD]
            dcs[n, PAD + R :] = out[PAD:]
        else:
            rows = jnp.concatenate([u[n, group * per + cc] for cc in range(per)], axis=1)
            dcs[n, PAD : PAD + R] = dot(rows, table).astype(bf16)


def stack_rows(buf, k, B):
    span = B + 2 * PAD
    return jnp.concatenate([buf[n, k * B : k * B + span] for n in range(NB)], axis=0)


def spill_rows(R, B, group, hrows, dcs, spout):
    for k in range(R // B):
        spout[group, :, k * B : k * B + B] = dot(hrows[...], stack_rows(dcs, k, B)).T.astype(bf16)


def place_sides(W, cc):
    row = lax.broadcasted_iota(jnp.int32, (W, W), 0)
    col = lax.broadcasted_iota(jnp.int32, (W, W), 1)
    rr = row % (W // 2)
    target = jnp.where(row < W // 2, 0, W - MARGIN) + rr % MARGIN
    return jnp.where((rr // MARGIN == cc) & (col == target), 1.0, 0.0).astype(bf16)


def pick_sides(W, cc):
    row = lax.broadcasted_iota(jnp.int32, (2 * MARGIN, W), 0)
    col = lax.broadcasted_iota(jnp.int32, (2 * MARGIN, W), 1)
    source = jnp.where(row < MARGIN, 0, W // 2 - MARGIN) + cc * MARGIN + row
    return jnp.where(col == source, 1.0, 0.0).astype(bf16)


def first_pair_cols(R, chans, u, gcols, dc):
    for n in range(NB):
        dc[n, PAD : PAD + R] = dot(
            jnp.concatenate([u[n, c] for c in chans], axis=1), gcols[n]
        ).astype(bf16)
        dc[n, :PAD] = jnp.zeros_like(dc[n, :PAD])
        dc[n, PAD + R :] = jnp.zeros_like(dc[n, PAD + R :])


def first_pair_halo(R, chans, up, lo, gcols, dc):
    for n in range(NB):
        top = jnp.concatenate([up[n, c] for c in chans], axis=1)
        bottom = jnp.concatenate([lo[n, c] for c in chans], axis=1)
        out = dot(jnp.concatenate([top, bottom], axis=0), gcols[n]).astype(bf16)
        dc[n, :PAD] = out[:PAD]
        dc[n, PAD + R :] = out[PAD:]


def first_pair_rows(W, B, k, hrows, dc, adj):
    start = pl.multiple_of(k * B, B)
    block = [dc[n, pl.ds(start, B + 2 * PAD)] for n in range(NB)]
    out = dot(hrows[...], jnp.concatenate(block, axis=0)).astype(bf16)
    for e in range(2):
        adj[e, pl.ds(start, B)] = out[:, e * W : (e + 1) * W]


def adjoint_pair(R, W, B, chans, u, up, lo, gcols, hrows, sides, dc, store):
    per = W // (2 * MARGIN)
    for n in range(NB):
        rows = [jnp.concatenate([up[n, c], u[n, c], lo[n, c]], axis=0) for c in chans]
        dc[n] = dot(jnp.concatenate(rows, axis=1), gcols[n]).astype(bf16)
    place = [place_sides(W, c % per) for c in chans]
    for k in range(R // B):
        out = dot(hrows[...], stack_rows(dc, k, B))
        for e, c in enumerate(chans):
            moved = dot(sides[c // per, k * B : k * B + B], place[e])
            store(e, k, (out[:, e * W : (e + 1) * W] + moved).astype(bf16))


def half_chunk(FC, x, colT, out, lanes):
    rows = jnp.concatenate([x[b] for b in range(FC)], axis=1)
    out[:, lanes] = dot(rows, colT[:, lanes]).astype(bf16)


def table_body(s, FR, R, colT, bown, aown, aoth):
    half = FR * R
    for a in range(FR):
        own = pl.ds(pl.multiple_of((2 * a + s) * R, R), R)
        bown[a * R : (a + 1) * R] = colT[own, :]
    odd_lane = lax.broadcasted_iota(jnp.int32, (1, half), 1) % 2 == 1
    flip = jnp.where(odd_lane & (s == 1), -1.0, 1.0).astype(f32)
    odd_row = lax.broadcasted_iota(jnp.int32, (half, 1), 0) % 2 == 1
    for dst, part in ((aown, s), (aoth, 1 - s)):
        for q in range(2):
            lanes = slice(q * half, (q + 1) * half)
            if FR == 1:
                sign = jnp.where(odd_row & (part == 1), -1.0, 1.0).astype(f32)
                dst[:, lanes] = (colT[:half, lanes].astype(f32) * (sign * flip)).astype(bf16)
                continue
            pieces = [
                colT[pl.ds(pl.multiple_of((2 * a + part) * R, R), R), lanes] for a in range(FR)
            ]
            block = jnp.concatenate(pieces, axis=0)
            dst[:, lanes] = (block.astype(f32).T * flip).astype(bf16)


def stack_re_im(ref, lanes_re, lanes_im, transpose):
    re, im = ref[:, lanes_re], ref[:, lanes_im]
    if transpose:
        return jnp.concatenate([re, im], 0), jnp.concatenate([im, -re], 0)
    return jnp.concatenate([re, -im], 0), jnp.concatenate([im, re], 0)


def vis_chunk(aown, aoth, hown, hoth, wts, out, re_l, im_l):
    own_re, own_im = stack_re_im(hown, re_l, im_l, False)
    oth_re, oth_im = stack_re_im(hoth, re_l, im_l, False)
    scale = weight_unit * wts[:, re_l].astype(f32)
    re = dot(aown[...], own_re) + dot(aoth[...], oth_re)
    out[:, re_l] = (scale * re).astype(bf16)
    im = dot(aown[...], own_im) + dot(aoth[...], oth_im)
    out[:, im_l] = (scale * im).astype(bf16)


def back_chunk(s, half, bown, wown, woth, out, re_l, im_l):
    odd = lax.broadcasted_iota(jnp.int32, (half, 1), 0) % 2 == 1
    own_sign = jnp.where(odd & (s == 1), -1.0, 1.0)
    oth_sign = jnp.where(odd & (s == 0), -1.0, 1.0)
    own_re, own_im = stack_re_im(wown, re_l, im_l, True)
    oth_re, oth_im = stack_re_im(woth, re_l, im_l, True)
    re = own_sign * dot(bown[...], own_re) + oth_sign * dot(bown[...], oth_re)
    out[:, re_l] = re.astype(bf16)
    im = own_sign * dot(bown[...], own_im) + oth_sign * dot(bown[...], oth_im)
    out[:, im_l] = im.astype(bf16)


def gradient_body(FC, W, back, colT, x, d, pre):
    step = 2 * W

    @pl.loop(0, FC // 2)
    def _(j):
        lanes = pl.ds(pl.multiple_of(j * step, step), step)
        grad = lax.dot_general(
            back[...], colT[lanes, :], (((1,), (1,)), ((), ())), preferred_element_type=f32
        )
        xs = jnp.concatenate([x[2 * j], x[2 * j + 1]], axis=1).astype(f32)
        ds = jnp.concatenate([d[2 * j], d[2 * j + 1]], axis=1).astype(f32)
        pre[:, lanes] = xs - primal_step * (grad - ds)


def forward_cols(R, W, c, block, fcols, ic):
    cut = min(R, W)
    sides = [block[c, R + at * PAD : R + at * PAD + PAD, :cut] for at in range(R // cut)]
    sides = jnp.concatenate(sides, axis=1) if len(sides) > 1 else sides[0]
    rows = jnp.concatenate([block[c, :R], sides.astype(f32).T.astype(bf16)], axis=1)
    out = dot(rows, fcols[...])
    lanes = pl.ds(pl.multiple_of(c * W, W), W)
    for n in range(NB):
        ic[n, PAD : PAD + R, lanes] = out[:, n * W : (n + 1) * W].astype(bf16)


def forward_rows(R, W, B, chans, first, ic, frows, u, total):
    span = B + 2 * PAD
    lanes = [pl.ds(pl.multiple_of(c * W, W), W) for c in chans]
    for n in range(NB):
        for k in range(R // B):
            rows = slice(k * B, (k + 1) * B)
            block = [ic[n, k * B : k * B + span, at] for at in lanes]
            coef = dot(frows[n], jnp.concatenate(block, axis=1) if len(block) > 1 else block[0])
            acc = None if first else total[n, rows]
            for e, c in enumerate(chans):
                st = u[n, c, rows].astype(f32) + dual_step * coef[:, e * W : (e + 1) * W]
                u[n, c, rows] = st.astype(bf16)
                acc = st * st if acc is None else acc + st * st
            total[n, rows] = acc


def shrink_body(C, R, W, B, st, total, mask, new_in, out_hbm, new_hbm, out, sem_new, sem):
    moved = pltpu.make_async_copy(new_in, new_hbm, sem_new)
    moved.start()
    copies = []
    for n in range(NB):
        for k in range(R // B):
            rows = slice(k * B, (k + 1) * B)
            keep = radius * mask[rows].astype(f32)
            scale = keep / jnp.maximum(jnp.sqrt(total[n, rows]), radius)
            for c in range(C):
                out[n, c, rows] = (st[n, c, rows].astype(f32) * scale).astype(bf16)
        copy = pltpu.make_async_copy(out.at[n], out_hbm.at[n], sem.at[n])
        copy.start()
        copies.append(copy)
    for copy in copies:
        copy.wait()
    moved.wait()


def step_kernel(
    C, FC, FR, R, W, B,
    u_hbm, x_hbm, d_hbm, wts_hbm, mask_hbm, colT_hbm, row_taps, col_taps,
    new, u, total, mask,
    x, d, wts, colT, gcols, gside, hrows, fcols, frows,
    up, lo, dc, dcs, spout, spin, sides, adj, radj, fix, rfix,
    hown, hoth, wown, woth, back, bown, aown, aoth, pre,
    ext, rmain, ic,
    send_u, recv_u, send_s, recv_s, send_a, recv_a, send_b, recv_b, send_f, recv_f,
    send_e, recv_e, send_p, recv_p, send_h, recv_h, load, load_u,
):
    half = FC * W // 2
    me = lax.axis_index("chan")
    s = lax.axis_index("split")
    ma, mb = me % FR, me // FR
    has_up = (ma > 0) | (s == 1)
    has_down = (ma < FR - 1) | (s == 0)
    partner = {"chan": me, "split": 1 - s}
    down_id = {"chan": (me + s) % C, "split": 1 - s}
    up_id = {"chan": (me + s + C - 1) % C, "split": 1 - s}
    left_id = {"chan": (me + C - FR) % C, "split": s}
    right_id = {"chan": (me + FR) % C, "split": s}
    per = W // (2 * MARGIN)
    groups = C // per
    early = FR == 1 and R > B

    def remote(src, dst, ssem, rsem, device):
        return pltpu.make_async_remote_copy(
            src_ref=src, dst_ref=dst, send_sem=ssem, recv_sem=rsem,
            device_id=device, device_id_type=pl.DeviceIdType.MESH,
        )

    loads = [
        pltpu.make_async_copy(a, b, load.at[i])
        for i, (a, b) in enumerate(
            [(x_hbm, x), (colT_hbm, colT), (wts_hbm, wts), (d_hbm, d), (mask_hbm, mask)]
        )
    ]

    def peer(i):
        return (me + C // 2 + (i + 1) // 2 * (1 - 2 * (i % 2))) % C

    def load_duals(i):
        c = peer(i)
        return pltpu.make_async_copy(u_hbm.at[:, c], u.at[:, c], load_u.at[i])

    @pl.loop(0, C)
    def _(i):
        load_duals(i).start()

    for copy in loads:
        copy.start()
    barrier = pltpu.get_barrier_semaphore()

    @pl.loop(1, C)
    def _(i):
        pl.semaphore_signal(
            barrier, inc=1, device_id={"chan": (me + i) % C, "split": s},
            device_id_type=pl.DeviceIdType.MESH,
        )

    pl.semaphore_signal(barrier, inc=1, device_id=partner, device_id_type=pl.DeviceIdType.MESH)
    if FR > 1:
        cross = jnp.where(s == 0, ma > 0, ma < FR - 1)
        cross_chan = jnp.where(s == 0, (me + C - 1) % C, (me + 1) % C)

        @pl.when(cross)
        def _():
            pl.semaphore_signal(
                barrier, inc=1, device_id={"chan": cross_chan, "split": 1 - s},
                device_id_type=pl.DeviceIdType.MESH,
            )
            pl.semaphore_wait(barrier, 1)

    adjoint_tables(W, B, row_taps, col_taps, gcols, gside, hrows)
    def swap(to_a, has_a, to_b, has_b):
        @pl.when(has_a)
        def _():
            to_a.start()

        @pl.when(has_b)
        def _():
            to_b.start()

        def finish():
            @pl.when(has_a)
            def _():
                to_a.wait_send()
                to_b.wait_recv()

            @pl.when(has_b)
            def _():
                to_b.wait_send()
                to_a.wait_recv()

        return finish

    def clear(ref, lacking):
        @pl.when(jnp.logical_not(lacking))
        def _():
            ref[...] = jnp.zeros_like(ref)

    clear(up, has_up)
    clear(lo, has_down)
    has_left, has_right = mb > 0, mb < FC - 1
    side_half = per * MARGIN
    clear(spin.at[:, pl.ds(0, side_half)], has_left)
    clear(spin.at[:, pl.ds(side_half, side_half)], has_right)

    def send_adjoint(i):
        return remote(
            adj.at[i], radj.at[me], send_a.at[i], recv_a.at[me], {"chan": peer(i), "split": s}
        )

    inner = pl.ds(pl.multiple_of(s * B, B), R - B)
    outer = pl.ds(pl.multiple_of((1 - s) * (R - B), B), B)

    def send_inner(i):
        return remote(
            adj.at[i, inner], radj.at[me, inner], send_a.at[i], recv_a.at[me],
            {"chan": peer(i), "split": s},
        )

    def send_outer(i):
        return remote(
            adj.at[i, outer], radj.at[me, outer], send_b.at[i], recv_b.at[i],
            {"chan": peer(i), "split": s},
        )

    def send_fix(i):
        return remote(
            fix.at[i], rfix.at[i], send_f.at[i], recv_f.at[i], {"chan": peer(i), "split": s}
        )

    def halo_duals(at, i):
        return swap(
            remote(
                u.at[:, at, pl.ds(R - PAD, PAD)], up.at[:, at], send_u.at[i], recv_u.at[i], down_id
            ), has_down,
            remote(
                u.at[:, at, pl.ds(0, PAD)], lo.at[:, at], send_u.at[C + i], recv_u.at[C + i], up_id
            ), has_up,
        )

    if early:
        firsts = (peer(0), peer(1))
        load_duals(0).wait()
        load_duals(1).wait()
        first_pair_cols(R, firsts, u, gcols, dc)
        last = R // B - 1
        for k in range(last):
            first_pair_rows(W, B, k + s, hrows, dc, adj)
        pl.semaphore_wait(barrier, C)
        send_inner(0).start()
        send_inner(1).start()
        side_tables(W, gside)
        halos = [halo_duals(firsts[i], i) for i in range(2)]
        for i in range(2, C):
            load_duals(i).wait()
            halos.append(halo_duals(peer(i), i))
        for g in range(groups):
            spill_cols(R, g, per, u, up, lo, gside, dcs.at[g], False)
        for finish in halos[:2]:
            finish()
        for finish in halos[2:]:
            finish()
        for g in range(groups):
            spill_cols(R, g, per, u, up, lo, gside, dcs.at[g], True)
            spill_rows(R, B, g, hrows, dcs.at[g], spout)
    else:
        side_tables(W, gside)

        @pl.loop(0, C)
        def _(i):
            load_duals(i).wait()

        pl.semaphore_wait(barrier, C)
        halo_duals(slice(None), 0)()

        @pl.loop(0, groups)
        def _(g):
            spill_cols(R, g, per, u, up, lo, gside, dcs.at[0], False)
            spill_cols(R, g, per, u, up, lo, gside, dcs.at[0], True)
            spill_rows(R, B, g, hrows, dcs.at[0], spout)

    finish_s = swap(
        remote(
            spout.at[:, pl.ds(0, side_half)], spin.at[:, pl.ds(side_half, side_half)],
            send_s.at[0], recv_s.at[0], left_id,
        ), has_left,
        remote(
            spout.at[:, pl.ds(side_half, side_half)], spin.at[:, pl.ds(0, side_half)],
            send_s.at[1], recv_s.at[1], right_id,
        ), has_right,
    )

    if early:
        first_pair_halo(R, firsts, up, lo, gcols, dc)
        first_pair_rows(W, B, last * (1 - s), hrows, dc, adj)
        send_outer(0).start()
        send_outer(1).start()

    step = 256
    chunks = half // step

    def to_partner(buf, dst, lanes, i):
        return remote(buf.at[:, lanes], dst.at[:, lanes], send_p.at[i], recv_p.at[i], partner)

    def parts(j):
        return pl.ds(j * step, step), pl.ds(half + j * step, step)

    loads[0].wait()
    loads[1].wait()
    copies = []
    for j in range(chunks):
        for q, lanes in enumerate(parts(j)):
            half_chunk(FC, x, colT, hown, lanes)
            copy = to_partner(hown, hoth, lanes, 2 * j + q)
            copy.start()
            copies.append(copy)

    table_body(s, FR, R, colT, bown, aown, aoth)
    finish_s()
    for g in range(groups):
        sides[g] = spin[g].astype(f32).T.astype(bf16)

    def adjoint_step(i):
        chans = (peer(i), peer(i + 1))

        def store(e, k, value):
            adj[i + e, k * B : k * B + B] = value

        adjoint_pair(R, W, B, chans, u, up, lo, gcols, hrows, sides, dc, store)
        send_adjoint(i).start()

        @pl.when(i + 1 < C - 1)
        def _():
            send_adjoint(i + 1).start()

        @pl.when(i + 1 == C - 1)
        def _():
            radj[me] = adj[C - 1]

    if early:
        for i, c in enumerate(firsts):
            fix[i] = dot(pick_sides(W, c % per), spin[c // per]).astype(bf16)
            send_fix(i).start()
        for i in range(2, C, 2):
            adjoint_step(i)
    else:
        @pl.loop(0, groups)
        def _(g):
            for pair in range(0, per, 2):
                adjoint_step(g * per + pair)

    for copy in loads[2:]:
        copy.wait()
    second = []
    for j in range(chunks):
        copies[2 * j].wait()
        copies[2 * j + 1].wait()
        vis_chunk(aown, aoth, hown, hoth, wts, wown, *parts(j))
        for q, lanes in enumerate(parts(j)):
            copy = to_partner(wown, woth, lanes, 2 * chunks + 2 * j + q)
            copy.start()
            second.append(copy)
    forward_tables(W, B, row_taps, col_taps, fcols, frows)
    clear(ic.at[:, pl.ds(0, PAD)], has_up)
    clear(ic.at[:, pl.ds(PAD + R, PAD)], has_down)
    for j in range(chunks):
        second[2 * j].wait()
        second[2 * j + 1].wait()
        back_chunk(s, half, bown, wown, woth, back, *parts(j))
    gradient_body(FC, W, back, colT, x, d, pre)

    k = lax.broadcasted_iota(jnp.int32, (2 * MARGIN, W), 0)
    col = lax.broadcasted_iota(jnp.int32, (2 * MARGIN, W), 1)
    take_left = jnp.where((k < MARGIN) & (col == W - MARGIN + k), 1.0, 0.0)
    put_back = jnp.where(col == jnp.where(k < MARGIN, k, W - 2 * MARGIN + k), 1.0, 0.0).astype(bf16)
    take_right = jnp.where((k >= MARGIN) & (col == k - MARGIN), 1.0, 0.0)

    def deliver(i, start):
        b = (mb + i) % FC
        for j in range(FR):
            f = b * FR + (ma + j) % FR
            r = i * FR + j
            if r == 0:
                if start:
                    rmain[me] = ext[f]
                continue
            copy = remote(
                ext.at[f], rmain.at[me], send_e.at[r], recv_e.at[r], {"chan": f, "split": s}
            )
            if start:
                copy.start()
            else:
                copy.wait_send()

    def image_cell(i):
        b = (mb + i) % FC
        at = order.index(i) - 1
        fixed = early and 0 <= at < 2
        for j in range(FR):
            if i or j:
                f = b * FR + (ma + j) % FR
                rows = inner if fixed else slice(None)
                remote(
                    adj.at[0, rows], radj.at[f, rows], send_a.at[0], recv_a.at[f], partner
                ).wait_recv()
        if fixed:
            send_outer(at).wait_recv()
            send_fix(at).wait_recv()
        lanes = pl.ds(pl.multiple_of(b * W, W), W)
        pieces = [radj[b * FR + a] for a in range(FR)]
        main = jnp.concatenate(pieces, axis=0) if FR > 1 else pieces[0]
        main = main.astype(f32)
        if fixed:
            main = main + lax.dot_general(
                rfix[at], put_back, (((0,), (0,)), ((), ())), preferred_element_type=f32
            )
        upd = pre[:, lanes] - primal_step * main
        nb = jnp.maximum(upd, 0.0).astype(bf16)
        eb = (2.0 * nb.astype(f32) - x[b].astype(f32)).astype(bf16)
        new[b] = nb
        for a in range(FR):
            ext[b * FR + a, :R] = eb[a * R : (a + 1) * R]

    cut = min(R, W)

    def image_sides(i):
        b = (mb + i) % FC
        left = jnp.where(b > 0, take_left, 0.0).astype(bf16)
        right = jnp.where(b < FC - 1, take_right, 0.0).astype(bf16)
        nt = (((1,), (1,)), ((), ()))
        for a in range(FR):
            lf = (b + FC - 1) % FC * FR + a
            rf = (b + 1) % FC * FR + a
            both = lax.dot_general(left, ext[lf, :R], nt, preferred_element_type=f32)
            both = both + lax.dot_general(right, ext[rf, :R], nt, preferred_element_type=f32)
            for at in range(R // cut):
                piece = both[:, at * cut : (at + 1) * cut].astype(bf16)
                ext[b * FR + a, R + at * PAD : R + at * PAD + PAD, :cut] = piece
        deliver(i, True)

    order = [0] + [FC // 2 - (i + 1) // 2 * (1 - 2 * (i % 2)) for i in range(FC - 1)]
    ready, sided = set(), []
    for i in order:
        image_cell(i)
        ready.add(i)
        for q in order:
            if q not in sided and {q, (q + 1) % FC, (q - 1) % FC} <= ready:
                image_sides(q)
                sided.append(q)

    def halo(c, i):
        lanes = pl.ds(pl.multiple_of(c * W, W), W)
        return swap(
            remote(
                ic.at[:, pl.ds(R, PAD), lanes], ic.at[:, pl.ds(0, PAD), lanes],
                send_h.at[i], recv_h.at[c], down_id,
            ), has_down,
            remote(
                ic.at[:, pl.ds(PAD, PAD), lanes], ic.at[:, pl.ds(PAD + R, PAD), lanes],
                send_h.at[C + i], recv_h.at[C + c], up_id,
            ), has_up,
        )

    sided.remove(0)
    arrivals = [(i, j) for i in [0] + sided for j in range(FR)]
    pending = []
    started = []

    def rows_of(count):
        batch = pending[:count]
        del pending[:count]
        for _, finish in batch:
            finish()
        forward_rows(R, W, B, [c for c, _ in batch], not started, ic, frows, u, total)
        started.append(True)

    for i, j in arrivals:
        r = i * FR + j
        src_b, src_a = (mb + FC - i) % FC, (ma + FR - j) % FR
        c = src_b * FR + src_a
        if r:
            device = {"chan": c, "split": s}
            remote(ext.at[c], rmain.at[c], send_e.at[r], recv_e.at[r], device).wait_recv()
        forward_cols(R, W, c, rmain, fcols, ic)
        pending.append((c, halo(c, r)))
        if FR == 1 and len(pending) > LAG:
            rows_of(1)
    while pending:
        rows_of(1 if FR == 1 else 2)

    for i in range(FC):
        deliver(i, False)

    if early:
        for i in range(2):
            send_inner(i).wait_send()
            send_outer(i).wait_send()
            send_fix(i).wait_send()

    @pl.loop(2 if early else 0, C - 1)
    def _(i):
        send_adjoint(i).wait_send()


def per_device(sky_image, dirty_image, uv_weights, dual_coeffs, support_mask, row_taps, col_taps):
    FC, FR = sky_image.shape[1], sky_image.shape[2]
    R, W = sky_image.shape[4], sky_image.shape[5]
    C = dual_coeffs.shape[1]
    npix = FC * W
    half = npix // 2
    B = min(128, R)
    RP = R + 2 * PAD
    per = W // (2 * MARGIN)
    u = dual_coeffs.reshape(NB, C, R, W)
    x = sky_image.reshape(FC, FR * R, W)
    d = dirty_image.reshape(FC, FR * R, W)
    wts = uv_weights.reshape(half, half)
    mask = support_mask.reshape(R, W)
    colT = col_dft(npix)
    vm = lambda *shape: pltpu.VMEM(shape, bf16)
    sem = lambda n: pltpu.SemaphoreType.DMA((n,))
    any_spec = pl.BlockSpec(memory_space=pl.ANY)
    smem_spec = pl.BlockSpec(memory_space=pltpu.SMEM)
    vmem_spec = pl.BlockSpec(memory_space=pltpu.VMEM)
    span = B + 2 * PAD
    extra = R // min(R, W) * PAD
    held = pl.pallas_call(
        functools.partial(step_kernel, C, FC, FR, R, W, B),
        out_shape=[
            vm(FC, FR * R, W), vm(NB, C, R, W), pltpu.VMEM((NB, R, W), f32),
            pltpu.VMEM((R, W), jnp.int32),
        ],
        in_specs=[any_spec] * 6 + [smem_spec] * 2,
        out_specs=[vmem_spec] * 4,
        scratch_shapes=[
            vm(FC, FR * R, W), vm(FC, FR * R, W), pltpu.VMEM((half, half), jnp.int32), vm(npix, npix),
            vm(NB, 2 * W, 2 * W), vm(NB, per * W, W), vm(B, NB * span), vm(W + 16, NB * W), vm(NB, B, span),
            vm(NB, C, PAD, W), vm(NB, C, PAD, W), vm(NB, RP, 2 * W),
            vm(C // per if FR == 1 else 1, NB, RP, W),
            vm(C // per, W, R), vm(C // per, W, R), vm(C // per, R, W), vm(C, R, W), vm(C, R, W),
            vm(2, 2 * MARGIN, R), vm(2, 2 * MARGIN, R),
            *[vm(half, npix)] * 8, pltpu.VMEM((half, npix), f32),
            vm(C, R + extra, W), vm(C, R + extra, W), vm(NB, RP, C * W),
            sem(2 * C), sem(2 * C), sem(2), sem(2), sem(C), sem(C), sem(2), sem(2), sem(2), sem(2),
            sem(C), sem(C), sem(4 * half // 128), sem(4 * half // 128),
            sem(2 * C), sem(2 * C), sem(5), sem(C),
        ],
        compiler_params=pltpu.CompilerParams(
            collective_id=0, has_side_effects=True, vmem_limit_bytes=50 * 2**20
        ),
    )(u, x, d, wts, mask, colT, row_taps, col_taps)
    new, steps, total, mask = [pltpu.with_memory_space_constraint(a, pltpu.VMEM) for a in held]

    new_dual, new = pl.pallas_call(
        functools.partial(shrink_body, C, R, W, B),
        in_specs=[vmem_spec] * 4,
        out_specs=[any_spec] * 2,
        out_shape=[
            jax.ShapeDtypeStruct((NB, C, R, W), bf16),
            jax.ShapeDtypeStruct((FC, FR * R, W), bf16),
        ],
        scratch_shapes=[vm(NB, C, R, W), pltpu.SemaphoreType.DMA, sem(NB)],
        compiler_params=pltpu.CompilerParams(vmem_limit_bytes=50 * 2**20),
    )(steps, total, mask, new)
    return (new.reshape(sky_image.shape), new_dual.reshape(dual_coeffs.shape))


def solution(mesh):
    placed = (
        P(("cube", "chan"), None, None, "split", None, None),
        P(("cube", "chan"), None, None, "split", None, None),
        P(("cube", "chan"), "split", None),
        P(None, "cube", "chan", "split", None, None),
        P("chan", "split", None, None),
        P(),
        P(),
    )
    return jax.shard_map(
        per_device,
        mesh=mesh,
        in_specs=placed,
        out_specs=(
            P(("cube", "chan"), None, None, "split", None, None),
            P(None, "cube", "chan", "split", None, None),
        ),
        check_vma=False,
    )
```
